512 devices in a mesh: gx: 32 (over x_hi, z, core), gy: 8 (over y), gz: 2 (over x_lo).
Axes of the slice: x: 4 (x_hi: 2, x_lo: 2; x = x_hi * 2 + x_lo), y: 8, z: 8, core: 2. Of those that a mesh axis runs over, the one named last changes fastest.
Arguments:
- fields: float32 [2, 4, 3, 16, 512, 1024], P(None, None, None, 'gz', 'gx', 'gy'), may hold values from -6 to 6
- material: int32 [16, 512, 1024], P('gz', 'gx', 'gy'), may hold values from 0 to 3
- pml_width: int32 [6], replicated, may hold values from 2 to 4
- eps_real: float32 [4], replicated, may hold values from 1 to 12
- eps_loss: float32 [4], replicated, may hold values from 0.05 to 1
- coeffs: float32 [2, 4, 4], replicated, may hold values from -3 to 3
- ritz: float32 [2, 4], replicated, may hold values from -4 to 4
Outputs:
- basis_new: float32 [2, 4, 3, 16, 512, 1024], P(None, None, None, 'gz', 'gx', 'gy')
- residual: float32 [2, 4, 3, 16, 512, 1024], P(None, None, None, 'gz', 'gx', 'gy')
- gram_out: float32 [2, 4, 4], replicated
The draws below stay inside these ranges and needn't reach their ends.
All inputs are finite; a program needn't handle non-finite values.
Results may differ from the reference program's by a relative error of at most 0.000078.
Values sent between devices are 32-bit elements; how exact they have to be, the bound alone decides.
A program may use at most 64 MiB of HBM per device.

```python
import math
import jax
import jax.numpy as jnp
from jax import lax

NV = 4
NMAT = 4
NX = 512
NY = 1024
NZ = 16


def draw_fields(key, part):
    first_key, second_key = jax.random.split(key)
    dimensions = (NV, 3, NZ, NX, NY)
    real_part = jnp.clip(jax.random.normal(first_key, dimensions, jnp.float32), -4.0, 4.0)
    imag_part = jnp.clip(jax.random.normal(second_key, dimensions, jnp.float32), -4.0, 4.0)
    envelope = (0.5 + jnp.arange(NX, dtype=jnp.float32) / NX)[:, None]
    return jnp.stack([real_part * envelope, 0.5 * imag_part * envelope])


def touch_ends(values, own_key, smallest, high):
    place = [jax.random.randint(jax.random.fold_in(own_key, axis), (), 0, length) for axis, length in enumerate(values.shape)]
    widest = values.shape.index(max(values.shape))
    next_to = place[:widest] + [(place[widest] + 1) % values.shape[widest]] + place[widest + 1:]
    return values.at[tuple(place)].set(smallest).at[tuple(next_to)].set(high)


def gaussian(own_key, shape, deviation, limit, kind=jnp.bfloat16):
    return jnp.clip(deviation * jax.random.normal(own_key, shape, jnp.float32), -limit, limit).astype(kind)


def setup_inputs(seed: int = 0) -> dict:
    seeds = jax.random.split(jax.random.key(seed), 8)
    return {
        "fields": draw_fields(jax.random.fold_in(seeds[7], 71), 0),
        "material": touch_ends(jax.random.randint(seeds[1], (NZ, NX, NY), 0, NMAT), jax.random.fold_in(seeds[1], 1), 0, NMAT - 1).astype(jnp.int32),
        "pml_width": touch_ends(jax.random.randint(seeds[2], (6,), 2, 5), jax.random.fold_in(seeds[2], 1), 2, 4).astype(jnp.int32),
        "eps_real": jnp.clip(jnp.exp(jax.random.uniform(seeds[3], (NMAT,), jnp.float32, math.log(1.0), math.log(12.0))), 1.0, 12.0),
        "eps_loss": jnp.clip(jax.random.uniform(seeds[4], (NMAT,), jnp.float32, 0.05, 1.0), 0.05, 1.0),
        "coeffs": gaussian(seeds[5], (2, NV, NV), 0.5, 3.0, jnp.float32),
        "ritz": gaussian(seeds[6], (2, NV), 1.0, 4.0, jnp.float32),
    }


OMEGA_SQ = 0.36
SIGMA_TOP = 3.0


def inverse_stretch(places, length, low_width, high_width):
    low_width = low_width.astype(jnp.float32)
    high_width = high_width.astype(jnp.float32)
    inside_depth = jnp.clip((low_width - places) / low_width, 0.0, 1.0) + jnp.clip((places + 1.0 - length + high_width) / high_width, 0.0, 1.0)
    absorb = SIGMA_TOP * inside_depth * inside_depth
    scaled = 1.0 / (1.0 + absorb * absorb)
    return jnp.stack([scaled, -absorb * scaled])


def complex_mul(factor, values):
    real_part = factor[0] * values[0] - factor[1] * values[1]
    imag_part = factor[0] * values[1] + factor[1] * values[0]
    return jnp.stack([real_part, imag_part])


def spread(factor, direction, rank):
    layout = [2] + [1] * (rank - 1)
    layout[rank - 3 + direction] = factor.shape[1]
    return factor.reshape(layout)


def curl_of(components, derivative):
    return [derivative(components[2], 2) - derivative(components[1], 0),
            derivative(components[0], 0) - derivative(components[2], 1),
            derivative(components[1], 1) - derivative(components[0], 2)]


def step_up(values, direction):
    where_dim = values.ndim - 3 + direction
    following = jnp.concatenate([lax.slice_in_dim(values, 1, values.shape[where_dim], axis=where_dim), jnp.zeros_like(lax.slice_in_dim(values, 0, 1, axis=where_dim))], axis=where_dim)
    return following - values


def step_down(values, direction):
    where_dim = values.ndim - 3 + direction
    previous = jnp.concatenate([jnp.zeros_like(lax.slice_in_dim(values, 0, 1, axis=where_dim)), lax.slice_in_dim(values, 0, values.shape[where_dim] - 1, axis=where_dim)], axis=where_dim)
    return values - previous


def operate(single_field, eps_cell, stretch_e, stretch_h):
    components = [single_field[:, number] for number in range(3)]
    magnetic = curl_of(components, lambda values, direction: complex_mul(spread(stretch_h[direction], direction, 4), step_up(values, direction)))
    electric = curl_of(magnetic, lambda values, direction: complex_mul(spread(stretch_e[direction], direction, 4), step_down(values, direction)))
    images = [electric[number] - OMEGA_SQ * complex_mul(eps_cell, components[number]) for number in range(3)]
    return jnp.stack(images, axis=1)


def product(left, right):
    return jnp.einsum('am,bm->ab', left, right, precision=lax.Precision.HIGHEST)


def bilinear(values, images):
    gram_re = product(values[0], images[0]) - product(values[1], images[1])
    gram_im = product(values[0], images[1]) + product(values[1], images[0])
    return gram_re, gram_im


def matmul_complex(left, right):
    high = lax.Precision.HIGHEST
    real_part = jnp.matmul(left[0], right[0], precision=high) - jnp.matmul(left[1], right[1], precision=high)
    imag_part = jnp.matmul(left[0], right[1], precision=high) + jnp.matmul(left[1], right[0], precision=high)
    return jnp.stack([real_part, imag_part])


def rotate_small(gram_full, coeffs):
    turned = jnp.stack([coeffs[0].T, coeffs[1].T])
    return matmul_complex(turned, matmul_complex(gram_full, coeffs))


def rotate(values, coeffs):
    high = lax.Precision.HIGHEST
    real_part = jnp.einsum('ab,am->bm', coeffs[0], values[0], precision=high) - jnp.einsum('ab,am->bm', coeffs[1], values[1], precision=high)
    imag_part = jnp.einsum('ab,am->bm', coeffs[0], values[1], precision=high) + jnp.einsum('ab,am->bm', coeffs[1], values[0], precision=high)
    return jnp.stack([real_part, imag_part])


def reference(fields, material, pml_width, eps_real, eps_loss, coeffs, ritz):
    lengths = (NZ, NX, NY)
    bounds = ((4, 5), (0, 1), (2, 3))
    stretch_e = []
    stretch_h = []
    for direction in range(3):
        length = lengths[direction]
        places = jnp.arange(length, dtype=jnp.int32).astype(jnp.float32)
        low_slot, high_slot = bounds[direction]
        stretch_e.append(inverse_stretch(places, jnp.float32(length), pml_width[low_slot], pml_width[high_slot]))
        stretch_h.append(inverse_stretch(places + 0.5, jnp.float32(length), pml_width[low_slot], pml_width[high_slot]))
    eps_re = jnp.zeros(material.shape, jnp.float32)
    eps_im = jnp.zeros(material.shape, jnp.float32)
    for number in range(NMAT):
        chosen = (material == number).astype(jnp.float32)
        eps_re = eps_re + eps_real[number] * chosen
        eps_im = eps_im + eps_loss[number] * chosen
    eps_cell = jnp.stack([eps_re, eps_im])
    images = lax.map(lambda single_field: operate(single_field, eps_cell, stretch_e, stretch_h), jnp.moveaxis(fields, 1, 0))
    images = jnp.moveaxis(images, 0, 1)
    values = fields.reshape(2, NV, -1)
    image_flat = images.reshape(2, NV, -1)
    gram_re, gram_im = bilinear(values, image_flat)
    weight_scale = 1.0 / (3.0 * NX * NY * NZ)
    gram_out = rotate_small(jnp.stack([gram_re, gram_im]), coeffs) * weight_scale
    basis_new = rotate(values, coeffs)
    rotated_image = rotate(image_flat, coeffs)
    residual = rotated_image - complex_mul(ritz[:, :, None], basis_new)
    return basis_new.reshape(fields.shape), residual.reshape(fields.shape), gram_out
```

```python
import functools

import jax
import jax.numpy as jnp
from jax import lax
from jax.experimental import pallas as pl
from jax.experimental.pallas import tpu as pltpu
from jax.sharding import Mesh
from jax.sharding import PartitionSpec as P

GX = ("xh", "zz", "core")
OMEGA_SQ = 0.36
SIGMA_TOP = 3.0
NV = 4
MESH = pl.DeviceIdType.MESH
PAIRS = [(a, b) for a in range(NV) for b in range(a, NV)]


def inverse_stretch(places, length, low_width, high_width):
    inside_depth = jnp.clip((low_width - places) / low_width, 0.0, 1.0) + jnp.clip(
        (places + 1.0 - length + high_width) / high_width, 0.0, 1.0
    )
    absorb = SIGMA_TOP * inside_depth * inside_depth
    scaled = 1.0 / (1.0 + absorb * absorb)
    return scaled, -absorb * scaled


def cmul(f, v):
    return (f[0] * v[0] - f[1] * v[1], f[0] * v[1] + f[1] * v[0])


def csub(p, q):
    return (p[0] - q[0], p[1] - q[1])


def curl(dx, dy, dz):
    return (
        csub(dy[2], dz[1]),
        csub(dz[0], dx[2]),
        csub(dx[1], dy[0]),
    )


def fold(x):
    return x[0:8] + x[8:16]


def kernel(
    sizes,
    pml_hbm, eps_r_hbm, eps_l_hbm, coef_hbm, ritz_hbm, mat_hbm, fields,
    basis, resid, gram,
    pml, eps_r, eps_l, coef, ritz, mat, v, h, gs, acc, sym, eps, sxy, sz,
    send_x, send_y, up_xh, up_yh, up_zh,
    hsend_x, hsend_y, dn_xh, dn_yh, dn_zh,
    buf1, buf2, buf3,
    small_sem, load_sem, halo_send, halo_recv, ss1, rs1, ss2, rs2, ss3, rs3,
):
    nz, nx, ny, n_gx, n_gy, n_gz, n_zz = sizes
    n_x = n_gx // (2 * n_zz)
    xh, zz, core = (lax.axis_index(name) for name in GX)
    gy, gz = lax.axis_index("gy"), lax.axis_index("gz")
    gx = (xh * n_zz + zz) * 2 + core
    n1 = n_x * n_gz * 2
    g1 = (xh * n_gz + gz) * 2 + core

    def gx_id(index):
        return {"xh": index // (2 * n_zz), "zz": (index // 2) % n_zz, "core": index % 2}

    def g1_id(index):
        return {"xh": index // (2 * n_gz), "gz": (index // 2) % n_gz, "core": index % 2}

    gx_up, gx_dn = (gx + 1) % n_gx, (gx + n_gx - 1) % n_gx
    gy_up, gy_dn = (gy + 1) % n_gy, (gy + n_gy - 1) % n_gy

    barrier = pltpu.get_barrier_semaphore()

    def greet(device_id):
        pl.semaphore_signal(barrier, inc=1, device_id=device_id, device_id_type=MESH)

    for d in range(1, n1):
        greet(g1_id((g1 + d) % n1))
    for d in range(1, n_gy):
        greet({"gy": (gy + d) % n_gy})
    for d in range(1, n_zz):
        greet({"zz": (zz + d) % n_zz})
    greet(gx_id(gx_up))
    greet(gx_id(gx_dn))
    greetings = n1 - 1 + n_gy - 1 + n_zz - 1 + 2

    smalls = [
        pltpu.make_async_copy(src, dst, small_sem.at[k])
        for k, (src, dst) in enumerate(
            (
                (coef_hbm, coef), (pml_hbm, pml), (eps_r_hbm, eps_r),
                (eps_l_hbm, eps_l), (ritz_hbm, ritz), (mat_hbm, mat),
            )
        )
    ]
    for copy in smalls:
        copy.start()

    def load(z):
        return pltpu.make_async_copy(
            fields.at[:, :, :, z], v.at[:, :, :, z], load_sem.at[z]
        )

    for z in range(nz):
        load(z).start()
    for copy in smalls:
        copy.wait()

    row16 = lax.broadcasted_iota(jnp.int32, (16, 128), 0)
    lane16 = lax.broadcasted_iota(jnp.int32, (16, 128), 1)
    lane8 = lax.broadcasted_iota(jnp.int32, (8, 128), 1)
    row8 = lax.broadcasted_iota(jnp.int32, (8, 128), 0)

    def width(slot):
        return jnp.full((8, 128), pml[slot], jnp.int32).astype(jnp.float32)

    def put(kind, places, length, low, high):
        value = inverse_stretch(places, float(length), low, high)
        sxy[kind, 0] = value[0]
        sxy[kind, 1] = value[1]

    px = (row16 + gx * nx).astype(jnp.float32)
    py = (lane16 + gy * ny).astype(jnp.float32)
    twice = lambda t: jnp.concatenate([t, t], axis=0)
    lx, hx_w, ly, hy_w = (twice(width(slot)) for slot in range(4))
    total_x, total_y, total_z = nx * n_gx, ny * n_gy, nz * n_gz
    put(0, px + 0.5, total_x, lx, hx_w)
    put(1, px, total_x, lx, hx_w)
    put(2, px + 1.0, total_x, lx, hx_w)
    put(3, py + 0.5, total_y, ly, hy_w)
    put(4, py, total_y, ly, hy_w)
    put(5, py + 1.0, total_y, ly, hy_w)
    lz, hz_w = width(4), width(5)

    def z_stretch(z, carry):
        places = jnp.full((8, 128), z + gz * nz, jnp.int32).astype(jnp.float32)
        for kind, shift in ((0, 0.5), (1, 0.0)):
            value = inverse_stretch(places + shift, float(total_z), lz, hz_w)
            sz[kind, 0, z] = value[0]
            sz[kind, 1, z] = value[1]
        return carry

    lax.fori_loop(0, nz + 1, z_stretch, 0)

    for c in range(2):
        for a in range(NV):
            for b in range(NV):
                acc[c, a, b] = jnp.zeros((8, 128), jnp.float32)
        for k in range(len(PAIRS)):
            sym[c, k] = jnp.zeros((8, 128), jnp.float32)

    def rotate(z, packed):
        load(z).wait()
        packed = list(packed)
        for comp in range(3):
            vr = [v[0, a, comp, z] for a in range(NV)]
            vi = [v[1, a, comp, z] for a in range(NV)]
            for b in range(NV):
                re = im = None
                for a in range(NV):
                    cr, ci = coef[0, a, b], coef[1, a, b]
                    pr = cr * vr[a] - ci * vi[a]
                    pi = cr * vi[a] + ci * vr[a]
                    re = pr if re is None else re + pr
                    im = pi if im is None else im + pi
                for c, value in ((0, re), (1, im)):
                    basis[c, b, comp, z] = value
                    if comp != 0:
                        send_x[c, b, comp - 1, pl.ds(z, 1), :] = value[0:1]
                    if comp != 1:
                        slot = comp // 2
                        for t in range(2):
                            place = (c * NV + b) * 16 + 2 * z + t
                            first = jnp.broadcast_to(value[8 * t : 8 * t + 8, 0:1], (8, 128))
                            packed[slot] = jnp.where(lane8 == place, first, packed[slot])
        return tuple(packed)

    zero8 = jnp.zeros((8, 128), jnp.float32)
    packed = lax.fori_loop(0, nz, rotate, (zero8, zero8))
    send_y[0] = packed[0]
    send_y[1] = packed[1]

    pl.semaphore_wait(barrier, greetings)

    def remote(src, dst, slot, device_id):
        return pltpu.make_async_remote_copy(
            src_ref=src, dst_ref=dst, send_sem=halo_send.at[slot], recv_sem=halo_recv.at[slot],
            device_id=device_id, device_id_type=MESH,
        )

    up_z = remote(basis.at[:, :, 0:2, 0], up_zh, 0, {"gz": 0})
    up_x = remote(send_x, up_xh, 1, gx_id(gx_dn))
    up_y = remote(send_y, up_yh, 2, {"gy": gy_dn})

    @pl.when(gz == 1)
    def _():
        up_z.start()

    up_x.start()
    up_y.start()

    def local_gram(z, carry):
        m = mat[z]

        def pick(table):
            low = jnp.where(m == 0, table[0], table[1])
            return OMEGA_SQ * jnp.where(m < 2, low, jnp.where(m == 2, table[2], table[3]))

        er, ei = pick(eps_r), pick(eps_l)
        eps[0, z] = er
        eps[1, z] = ei
        for a in range(NV):
            q = [cmul((er, ei), (basis[0, a, comp, z], basis[1, a, comp, z])) for comp in range(3)]
            for b in range(a, NV):
                k = PAIRS.index((a, b))
                re = im = None
                for comp in range(3):
                    pr, pi = cmul(q[comp], (basis[0, b, comp, z], basis[1, b, comp, z]))
                    re = pr if re is None else re + pr
                    im = pi if im is None else im + pi
                sym[0, k] += fold(re)
                sym[1, k] += fold(im)
        return carry

    lax.fori_loop(0, nz, local_gram, 0)

    up_x.wait_recv()
    up_y.wait_recv()

    @pl.when(gx == n_gx - 1)
    def _():
        up_xh[...] = jnp.zeros(up_xh.shape, jnp.float32)

    @pl.when(gy == n_gy - 1)
    def _():
        up_yh[...] = jnp.zeros(up_yh.shape, jnp.float32)

    def pair(ref, *index):
        return ref[(0,) + index], ref[(1,) + index]

    def stretch(kind):
        return sxy[kind, 0], sxy[kind, 1]

    def stretch_z(kind, z):
        return twice(sz[kind, 0, z]), twice(sz[kind, 1, z])

    def unpacked(ref, slot, c, b, z, lane):
        parts = []
        for t in range(2):
            place = (c * NV + b) * 16 + 2 * z + t
            parts.append(pltpu.roll(ref[slot], (lane - place) % 128, 1))
        return jnp.concatenate(parts, axis=0)

    def forward(z, next_z):
        for b in range(NV):
            f = [pair(basis, b, comp, z) for comp in range(3)]

            def both(comp, ahead, sh, se, se_next):
                d = csub(ahead, f[comp])
                return cmul(sh, d), csub(cmul(se_next, ahead), cmul(se, f[comp]))

            dx, dy, dz = {}, {}, {}
            for comp in (1, 2):
                ahead = tuple(
                    jnp.where(
                        row16 == 15,
                        up_xh[c, b, comp - 1, pl.ds(z, 1), :],
                        pltpu.roll(f[comp][c], 15, 0),
                    )
                    for c in range(2)
                )
                dx[comp] = both(comp, ahead, stretch(0), stretch(1), stretch(2))
            for comp in (0, 2):
                ahead = tuple(
                    jnp.where(
                        lane16 == 127,
                        unpacked(up_yh, comp // 2, c, b, z, 127),
                        pltpu.roll(f[comp][c], 127, 1),
                    )
                    for c in range(2)
                )
                dy[comp] = both(comp, ahead, stretch(3), stretch(4), stretch(5))
            for comp in (0, 1):
                ahead = next_z(b, comp)
                dz[comp] = both(
                    comp, ahead, stretch_z(0, z), stretch_z(1, z), stretch_z(1, z + 1)
                )
            for part, where in ((0, "h"), (1, "g")):
                turned = curl(*({k: t[part] for k, t in d.items()} for d in (dx, dy, dz)))
                for comp in range(3):
                    for c in range(2):
                        if where == "h":
                            h[c, b, comp, z] = turned[comp][c]
                        else:
                            gs[c, b, comp] = turned[comp][c]
        for b in range(NV):
            hb = [pair(h, b, comp, z) for comp in range(3)]
            for a in range(NV):
                re = im = None
                for comp in range(3):
                    pr, pi = cmul(pair(gs, a, comp), hb[comp])
                    re = pr if re is None else re + pr
                    im = pi if im is None else im + pi
                acc[0, a, b] += fold(re)
                acc[1, a, b] += fold(im)

    def forward_step(z, carry):
        forward(z, lambda b, comp: pair(basis, b, comp, z + 1))
        return carry

    lax.fori_loop(0, nz - 1, forward_step, 0)

    @pl.when(gz == 0)
    def _():
        up_z.wait_recv()

    @pl.when(gz == 1)
    def _():
        up_zh[...] = jnp.zeros(up_zh.shape, jnp.float32)

    forward(nz - 1, lambda b, comp: pair(up_zh, b, comp))

    tile = zero8
    for b in range(NV):
        rows = zero8
        for c in range(2):
            for a in range(NV):
                s = acc[c, a, b] - sym[c, PAIRS.index((min(a, b), max(a, b)))]
                s = jnp.sum(s, axis=0, keepdims=True)
                rows = jnp.where(row8 == c * NV + a, s, rows)
        total = jnp.sum(rows, axis=1, keepdims=True)
        tile = jnp.where(lane8 == b, total, tile)

    def exchange(buf, count, me, ids, ss, rs):
        copies = []
        for d in range(1, count):
            peer = (me + d) % count
            copies.append(
                pltpu.make_async_remote_copy(
                    src_ref=buf.at[me], dst_ref=buf.at[me], send_sem=ss.at[d], recv_sem=rs.at[me],
                    device_id=ids(peer), device_id_type=MESH,
                )
            )
        for copy in copies:
            copy.start()

        def arrived():
            for d in range(1, count):
                peer = (me + d) % count
                pltpu.make_async_remote_copy(
                    src_ref=buf.at[peer], dst_ref=buf.at[peer], send_sem=ss.at[d],
                    recv_sem=rs.at[peer], device_id=ids(peer), device_id_type=MESH,
                ).wait_recv()
            total = buf[0]
            for k in range(1, count):
                total = total + buf[k]
            return total

        def sent():
            for copy in copies:
                copy.wait_send()

        return arrived, sent

    buf1[g1] = tile
    arrived1, sent1 = exchange(buf1, n1, g1, g1_id, ss1, rs1)

    def pack(z, packed):
        packed = list(packed)
        for b in range(NV):
            for c in range(2):
                for comp in range(3):
                    value = h[c, b, comp, z]
                    if comp != 0:
                        hsend_x[c, b, comp - 1, pl.ds(z, 1), :] = value[15:16]
                    if comp != 1:
                        slot = comp // 2
                        for t in range(2):
                            place = (c * NV + b) * 16 + 2 * z + t
                            last = jnp.broadcast_to(value[8 * t : 8 * t + 8, 127:128], (8, 128))
                            packed[slot] = jnp.where(lane8 == place, last, packed[slot])
        return tuple(packed)

    packed = lax.fori_loop(0, nz, pack, (zero8, zero8))
    hsend_y[0] = packed[0]
    hsend_y[1] = packed[1]
    dn_z = remote(h.at[:, :, 0:2, nz - 1], dn_zh, 3, {"gz": 1})
    dn_x = remote(hsend_x, dn_xh, 4, gx_id(gx_up))
    dn_y = remote(hsend_y, dn_yh, 5, {"gy": gy_up})

    @pl.when(gz == 0)
    def _():
        dn_z.start()

    dn_x.start()
    dn_y.start()

    buf2[gy] = arrived1()
    arrived2, sent2 = exchange(buf2, n_gy, gy, lambda k: {"gy": k}, ss2, rs2)

    dn_x.wait_recv()
    dn_y.wait_recv()

    @pl.when(gz == 1)
    def _():
        dn_z.wait_recv()

    @pl.when(gz == 0)
    def _():
        dn_zh[...] = jnp.zeros(dn_zh.shape, jnp.float32)

    @pl.when(gx == 0)
    def _():
        dn_xh[...] = jnp.zeros(dn_xh.shape, jnp.float32)

    @pl.when(gy == 0)
    def _():
        dn_yh[...] = jnp.zeros(dn_yh.shape, jnp.float32)

    def backward(z, behind_z):
        er, ei = eps[0, z], eps[1, z]
        for b in range(NV):
            f = [pair(h, b, comp, z) for comp in range(3)]
            dx, dy, dz = {}, {}, {}
            for comp in (1, 2):
                behind = tuple(
                    jnp.where(
                        row16 == 0,
                        dn_xh[c, b, comp - 1, pl.ds(z, 1), :],
                        pltpu.roll(f[comp][c], 1, 0),
                    )
                    for c in range(2)
                )
                dx[comp] = cmul(stretch(1), csub(f[comp], behind))
            for comp in (0, 2):
                behind = tuple(
                    jnp.where(
                        lane16 == 0,
                        unpacked(dn_yh, comp // 2, c, b, z, 128),
                        pltpu.roll(f[comp][c], 1, 1),
                    )
                    for c in range(2)
                )
                dy[comp] = cmul(stretch(4), csub(f[comp], behind))
            for comp in (0, 1):
                dz[comp] = cmul(stretch_z(1, z), csub(f[comp], behind_z(b, comp)))
            turned = curl(dx, dy, dz)
            shifted = (er + ritz[0, b], ei + ritz[1, b])
            for comp in range(3):
                out = csub(turned[comp], cmul(shifted, pair(basis, b, comp, z)))
                resid[0, b, comp, z] = out[0]
                resid[1, b, comp, z] = out[1]

    backward(0, lambda b, comp: pair(dn_zh, b, comp))

    def backward_step(z, carry):
        backward(z, lambda b, comp: pair(h, b, comp, z - 1))
        return carry

    lax.fori_loop(1, nz, backward_step, 0)

    buf3[zz] = arrived2()
    arrived3, sent3 = exchange(buf3, n_zz, zz, lambda k: {"zz": k}, ss3, rs3)

    @pl.when(gz == 1)
    def _():
        up_z.wait_send()

    @pl.when(gz == 0)
    def _():
        dn_z.wait_send()

    for copy in (up_x, up_y, dn_x, dn_y):
        copy.wait_send()
    sent1()
    sent2()
    final = arrived3() * (1.0 / (3.0 * total_x * total_y * total_z))
    gram[0] = final[0:NV, 0:NV]
    gram[1] = final[NV : 2 * NV, 0:NV]
    sent3()


def body(sizes, fields, material, pml_width, eps_real, eps_loss, coeffs, ritz):
    nz, nx, ny, n_gx, n_gy, n_gz, n_zz = sizes
    n1 = n_gx // n_zz * n_gz
    whole = fields.shape
    f32 = jnp.float32
    vmem = pl.BlockSpec(memory_space=pltpu.VMEM)
    face_x = pltpu.VMEM((2, NV, 2, nz, ny), f32)
    face_y = pltpu.VMEM((2, 8, 128), f32)
    face_z = pltpu.VMEM((2, NV, 2, nx, ny), f32)
    dma = pltpu.SemaphoreType.DMA
    return pl.pallas_call(
        functools.partial(kernel, sizes),
        out_shape=(
            jax.ShapeDtypeStruct(whole, f32),
            jax.ShapeDtypeStruct(whole, f32),
            jax.ShapeDtypeStruct((2, NV, NV), f32),
        ),
        in_specs=[pl.BlockSpec(memory_space=pltpu.HBM)] * 7,
        out_specs=(vmem, vmem, vmem),
        scratch_shapes=[
            pltpu.SMEM((6,), jnp.int32),
            pltpu.SMEM((4,), f32),
            pltpu.SMEM((4,), f32),
            pltpu.SMEM((2, NV, NV), f32),
            pltpu.SMEM((2, NV), f32),
            pltpu.VMEM((nz, nx, ny), jnp.int32),
            pltpu.VMEM(whole, f32),
            pltpu.VMEM(whole, f32),
            pltpu.VMEM((2, NV, 3, nx, ny), f32),
            pltpu.VMEM((2, NV, NV, 8, 128), f32),
            pltpu.VMEM((2, len(PAIRS), 8, 128), f32),
            pltpu.VMEM((2, nz, nx, ny), f32),
            pltpu.VMEM((6, 2, nx, ny), f32),
            pltpu.VMEM((2, 2, nz + 1, 8, 128), f32),
            face_x, face_y, face_x, face_y, face_z,
            face_x, face_y, face_x, face_y, face_z,
            pltpu.VMEM((n1, 8, 128), f32),
            pltpu.VMEM((n_gy, 8, 128), f32),
            pltpu.VMEM((n_zz, 8, 128), f32),
            dma((6,)),
            dma((nz,)),
            dma((6,)),
            dma((6,)),
            dma((n1,)), dma((n1,)),
            dma((n_gy,)), dma((n_gy,)),
            dma((n_zz,)), dma((n_zz,)),
        ],
        compiler_params=pltpu.CompilerParams(
            collective_id=0, has_side_effects=True, vmem_limit_bytes=24 * 1024 * 1024
        ),
    )(*(pltpu.with_memory_space_constraint(x, pltpu.HBM) for x in (pml_width, eps_real, eps_loss, coeffs, ritz, material, fields)))


def solution(mesh):
    n_gx, n_gy, n_gz = mesh.shape["gx"], mesh.shape["gy"], mesh.shape["gz"]
    n_zz = n_gx // 4
    split = Mesh(
        mesh.devices.reshape(2, n_zz, 2, n_gy, n_gz),
        ("xh", "zz", "core", "gy", "gz"),
    )
    sizes = (16 // n_gz, 512 // n_gx, 1024 // n_gy, n_gx, n_gy, n_gz, n_zz)
    placed = (P(None, None, None, "gz", GX, "gy"), P("gz", GX, "gy"), P(), P(), P(), P(), P())
    return jax.shard_map(
        functools.partial(body, sizes),
        mesh=split,
        in_specs=placed,
        out_specs=(P(None, None, None, "gz", GX, "gy"), P(None, None, None, "gz", GX, "gy"), P()),
        check_vma=False,
    )
```

```python
import functools

import jax
import jax.numpy as jnp
from jax import lax
from jax.experimental import pallas as pl
from jax.experimental.pallas import tpu as pltpu
from jax.sharding import Mesh
from jax.sharding import PartitionSpec as P

GX = ("xh", "zz", "core")
OMEGA_SQ = 0.36
SIGMA_TOP = 3.0
NV = 4
MESH = pl.DeviceIdType.MESH
PAIRS = [(a, b) for a in range(NV) for b in range(a, NV)]


def inverse_stretch(places, length, low_width, high_width):
    inside_depth = jnp.clip((low_width - places) / low_width, 0.0, 1.0) + jnp.clip(
        (places + 1.0 - length + high_width) / high_width, 0.0, 1.0
    )
    absorb = SIGMA_TOP * inside_depth * inside_depth
    scaled = 1.0 / (1.0 + absorb * absorb)
    return scaled, -absorb * scaled


def cmul(f, v):
    return (f[0] * v[0] - f[1] * v[1], f[0] * v[1] + f[1] * v[0])


def csub(p, q):
    return (p[0] - q[0], p[1] - q[1])


def curl(dx, dy, dz):
    return (
        csub(dy[2], dz[1]),
        csub(dz[0], dx[2]),
        csub(dx[1], dy[0]),
    )


def fold(x):
    return x[0:8] + x[8:16]


def kernel(
    sizes,
    pml_hbm, eps_r_hbm, eps_l_hbm, coef_hbm, ritz_hbm, mat_hbm, fields,
    basis, resid, gram,
    pml, eps_r, eps_l, coef, ritz, mat, v, h, gs, acc, sym, eps, sxy, sz,
    send_x, send_y, up_xh, up_yh, up_raw, up_zh,
    hsend_x, hsend_y, dn_xh, dn_yh, dn_zh,
    buf1, buf2, buf3,
    small_sem, load_sem, halo_send, halo_recv, ss1, rs1, ss2, rs2, ss3, rs3, near, far,
):
    nz, nx, ny, n_gx, n_gy, n_gz, n_zz = sizes
    n_x = n_gx // (2 * n_zz)
    xh, zz, core = (lax.axis_index(name) for name in GX)
    gy, gz = lax.axis_index("gy"), lax.axis_index("gz")
    gx = (xh * n_zz + zz) * 2 + core
    n1 = n_x * n_gz * 2
    g1 = (xh * n_gz + gz) * 2 + core

    def gx_id(index):
        return {"xh": index // (2 * n_zz), "zz": (index // 2) % n_zz, "core": index % 2}

    def g1_id(index):
        return {"xh": index // (2 * n_gz), "gz": (index // 2) % n_gz, "core": index % 2}

    gx_up, gx_dn = (gx + 1) % n_gx, (gx + n_gx - 1) % n_gx
    gy_up, gy_dn = (gy + 1) % n_gy, (gy + n_gy - 1) % n_gy

    smalls = [
        pltpu.make_async_copy(src, dst, small_sem.at[k])
        for k, (src, dst) in enumerate(
            (
                (coef_hbm, coef), (pml_hbm, pml), (eps_r_hbm, eps_r),
                (eps_l_hbm, eps_l), (ritz_hbm, ritz), (mat_hbm, mat),
            )
        )
    ]
    for copy in smalls:
        copy.start()

    for c in range(2):
        for a in range(NV):
            pltpu.make_async_copy(fields.at[c, a], v.at[c, a], load_sem).start()

    barrier = pltpu.get_barrier_semaphore()

    def signal(sem, device_id):
        pl.semaphore_signal(sem, inc=1, device_id=device_id, device_id_type=MESH)

    def beside(step):
        return (
            {"gy": (gy + step) % n_gy},
            {"gy": (gy + n_gy - step) % n_gy},
            {"zz": (zz + step) % n_zz},
            {"zz": (zz + n_zz - step) % n_zz},
        )

    greeted = [gx_id(gx_up), gx_id(gx_dn)] + list(beside(1))
    greeted += [g1_id((g1 + d) % n1) for d in range(1, n1)]
    for device_id in greeted:
        signal(barrier, device_id)

    def remote(src, dst, slot, device_id):
        return pltpu.make_async_remote_copy(
            src_ref=src, dst_ref=dst, send_sem=halo_send.at[slot], recv_sem=halo_recv.at[slot],
            device_id=device_id, device_id_type=MESH,
        )

    up_z = remote(fields.at[:, :, 0:2, 0], up_raw, 0, {"gz": 0})
    up_x = remote(send_x, up_xh, 1, gx_id(gx_dn))
    up_y = remote(send_y, up_yh, 2, {"gy": gy_dn})

    pl.semaphore_wait(barrier, len(greeted))

    @pl.when(gz == 1)
    def _():
        up_z.start()
        up_raw[...] = jnp.zeros(up_raw.shape, jnp.float32)

    for copy in smalls:
        copy.wait()

    for device_id in beside(1):
        signal(near, device_id)

    row16 = lax.broadcasted_iota(jnp.int32, (16, 128), 0)
    lane16 = lax.broadcasted_iota(jnp.int32, (16, 128), 1)
    lane8 = lax.broadcasted_iota(jnp.int32, (8, 128), 1)
    row8 = lax.broadcasted_iota(jnp.int32, (8, 128), 0)

    def width(slot):
        return jnp.full((8, 128), pml[slot], jnp.int32).astype(jnp.float32)

    def put(kind, places, length, low, high):
        value = inverse_stretch(places, float(length), low, high)
        sxy[kind, 0] = value[0]
        sxy[kind, 1] = value[1]

    px = (row16 + gx * nx).astype(jnp.float32)
    py = (lane16 + gy * ny).astype(jnp.float32)
    twice = lambda t: jnp.concatenate([t, t], axis=0)
    lx, hx_w, ly, hy_w = (twice(width(slot)) for slot in range(4))
    total_x, total_y, total_z = nx * n_gx, ny * n_gy, nz * n_gz
    put(0, px + 0.5, total_x, lx, hx_w)
    put(1, px, total_x, lx, hx_w)
    put(2, px + 1.0, total_x, lx, hx_w)
    put(3, py + 0.5, total_y, ly, hy_w)
    put(4, py, total_y, ly, hy_w)
    put(5, py + 1.0, total_y, ly, hy_w)
    lz, hz_w = width(4), width(5)

    def z_stretch(z, carry):
        places = jnp.full((8, 128), z + gz * nz, jnp.int32).astype(jnp.float32)
        for kind, shift in ((0, 0.5), (1, 0.0)):
            value = inverse_stretch(places + shift, float(total_z), lz, hz_w)
            sz[kind, 0, z] = value[0]
            sz[kind, 1, z] = value[1]
        return carry

    lax.fori_loop(0, nz + 1, z_stretch, 0)

    acc[...] = jnp.zeros(acc.shape, jnp.float32)
    sym[...] = jnp.zeros(sym.shape, jnp.float32)
    zero8 = jnp.zeros((8, 128), jnp.float32)

    pltpu.make_async_copy(fields, v, load_sem).wait()

    def combine(vr, vi, b):
        re = im = None
        for a in range(NV):
            cr, ci = coef[0, a, b], coef[1, a, b]
            pr = cr * vr[a] - ci * vi[a]
            pi = cr * vi[a] + ci * vr[a]
            re = pr if re is None else re + pr
            im = pi if im is None else im + pi
        return re, im

    def packed_lanes(ref, comp, lane):
        tile = None
        for c in range(2):
            for a in range(NV):
                part = None
                for z in range(nz):
                    for t in range(2):
                        column = ref[c, a, comp, z, 8 * t : 8 * t + 8, lane : lane + 1]
                        column = jnp.broadcast_to(column, (8, 128))
                        place = 2 * z + t
                        part = column if part is None else jnp.where(lane_in == place, column, part)
                group = c * NV + a
                tile = part if tile is None else jnp.where(lane_group == group, part, tile)
        return tile

    lane_in, lane_group = lane8 % 16, lane8 // 16
    factors = []
    for d in range(8):
        factor = None
        for out in range(8):
            src = (out - d) % 8
            a, b = src % NV, out % NV
            if out // NV == src // NV:
                value = coef[0, a, b]
            elif out // NV == 0:
                value = -coef[1, a, b]
            else:
                value = coef[1, a, b]
            factor = (
                jnp.full((8, 128), value, jnp.float32)
                if factor is None
                else jnp.where(lane_group == out, value, factor)
            )
        factors.append(factor)
    for slot, comp in ((0, 0), (1, 2)):
        raw = packed_lanes(v, comp, 0)
        turned = factors[0] * raw
        for d in range(1, 8):
            turned = turned + factors[d] * pltpu.roll(raw, 16 * d, 1)
        send_y[slot] = turned
    up_y.start()

    for comp in (1, 2):
        rows = [
            [
                jnp.concatenate([v[c, a, comp, z, 0:1, :] for z in range(nz)], axis=0)
                for a in range(NV)
            ]
            for c in range(2)
        ]
        for b in range(NV):
            re, im = combine(rows[0], rows[1], b)
            send_x[0, b, comp - 1] = re
            send_x[1, b, comp - 1] = im
    up_x.start()

    def rotate(z, carry):
        for comp in range(3):
            vr = [v[0, a, comp, z] for a in range(NV)]
            vi = [v[1, a, comp, z] for a in range(NV)]
            for b in range(NV):
                re, im = combine(vr, vi, b)
                basis[0, b, comp, z] = re
                basis[1, b, comp, z] = im
        return carry

    lax.fori_loop(0, nz, rotate, 0)

    def pair(ref, *index):
        return ref[(0,) + index], ref[(1,) + index]

    def three(value):
        return value[0], value[1], value[0] + value[1]

    def dot3(left, right):
        sums = None
        for p, q in zip(left, right):
            terms = [x * y for x, y in zip(p, q)]
            sums = terms if sums is None else [x + y for x, y in zip(sums, terms)]
        return sums

    def local_gram(z, carry):
        m = mat[z]

        def pick(table):
            low = jnp.where(m == 0, table[0], table[1])
            return OMEGA_SQ * jnp.where(m < 2, low, jnp.where(m == 2, table[2], table[3]))

        er, ei = pick(eps_r), pick(eps_l)
        eps[0, z] = er
        eps[1, z] = ei
        for a in range(NV):
            q = [three(cmul((er, ei), pair(basis, a, comp, z))) for comp in range(3)]
            for b in range(a, NV):
                k = PAIRS.index((a, b))
                for part, value in enumerate(dot3(q, [three(pair(basis, b, comp, z)) for comp in range(3)])):
                    sym[part, k] += fold(value)
        return carry

    lax.fori_loop(0, nz, local_gram, 0)

    pl.semaphore_wait(near, 4)
    for device_id in beside(2):
        signal(far, device_id)

    up_x.wait_recv()
    up_y.wait_recv()

    @pl.when(gx == n_gx - 1)
    def _():
        up_xh[...] = jnp.zeros(up_xh.shape, jnp.float32)

    @pl.when(gy == n_gy - 1)
    def _():
        up_yh[...] = jnp.zeros(up_yh.shape, jnp.float32)

    def stretch(kind):
        return sxy[kind, 0], sxy[kind, 1]

    def stretch_z(kind, z):
        return twice(sz[kind, 0, z]), twice(sz[kind, 1, z])

    def unpacked(ref, slot, c, b, z, lane):
        parts = []
        for t in range(2):
            place = (c * NV + b) * 16 + 2 * z + t
            parts.append(pltpu.roll(ref[slot], (lane - place) % 128, 1))
        return jnp.concatenate(parts, axis=0)

    def forward(z, next_z):
        for b in range(NV):
            f = [pair(basis, b, comp, z) for comp in range(3)]

            def both(comp, ahead, sh, se, se_next):
                d = csub(ahead, f[comp])
                return cmul(sh, d), csub(cmul(se_next, ahead), cmul(se, f[comp]))

            dx, dy, dz = {}, {}, {}
            for comp in (1, 2):
                ahead = tuple(
                    jnp.where(
                        row16 == 15,
                        up_xh[c, b, comp - 1, pl.ds(z, 1), :],
                        pltpu.roll(f[comp][c], 15, 0),
                    )
                    for c in range(2)
                )
                dx[comp] = both(comp, ahead, stretch(0), stretch(1), stretch(2))
            for comp in (0, 2):
                ahead = tuple(
                    jnp.where(
                        lane16 == 127,
                        unpacked(up_yh, comp // 2, c, b, z, 127),
                        pltpu.roll(f[comp][c], 127, 1),
                    )
                    for c in range(2)
                )
                dy[comp] = both(comp, ahead, stretch(3), stretch(4), stretch(5))
            for comp in (0, 1):
                ahead = next_z(b, comp)
                dz[comp] = both(
                    comp, ahead, stretch_z(0, z), stretch_z(1, z), stretch_z(1, z + 1)
                )
            for part, where in ((0, "h"), (1, "g")):
                turned = curl(*({k: t[part] for k, t in d.items()} for d in (dx, dy, dz)))
                for comp in range(3):
                    for c in range(2):
                        if where == "h":
                            h[c, b, comp, z] = turned[comp][c]
                        else:
                            gs[c, b, comp] = turned[comp][c]
                    if where == "g":
                        gs[2, b, comp] = turned[comp][0] + turned[comp][1]
        for b in range(NV):
            hb = [three(pair(h, b, comp, z)) for comp in range(3)]
            for a in range(NV):
                ga = [(gs[0, a, comp], gs[1, a, comp], gs[2, a, comp]) for comp in range(3)]
                for part, value in enumerate(dot3(ga, hb)):
                    acc[part, a, b] += fold(value)

    def forward_step(z, carry):
        forward(z, lambda b, comp: pair(basis, b, comp, z + 1))
        return carry

    lax.fori_loop(0, nz - 1, forward_step, 0)

    @pl.when(gz == 0)
    def _():
        up_z.wait_recv()

    for comp in range(2):
        vr = [up_raw[0, a, comp] for a in range(NV)]
        vi = [up_raw[1, a, comp] for a in range(NV)]
        for b in range(NV):
            up_zh[0, b, comp], up_zh[1, b, comp] = combine(vr, vi, b)

    forward(nz - 1, lambda b, comp: pair(up_zh, b, comp))

    tile = zero8
    for b in range(NV):
        rows = zero8
        for c in range(2):
            for a in range(NV):
                k = PAIRS.index((min(a, b), max(a, b)))
                sums = [acc[part, a, b] - sym[part, k] for part in range(3)]
                s = sums[0] - sums[1] if c == 0 else sums[2] - sums[0] - sums[1]
                s = jnp.sum(s, axis=0, keepdims=True)
                rows = jnp.where(row8 == c * NV + a, s, rows)
        total = jnp.sum(rows, axis=1, keepdims=True)
        tile = jnp.where(lane8 == b, total, tile)

    def exchange(buf, count, me, ids, ss, rs):
        for d in range(1, count):
            pltpu.make_async_remote_copy(
                src_ref=buf.at[me], dst_ref=buf.at[me], send_sem=ss, recv_sem=rs,
                device_id=ids((me + d) % count), device_id_type=MESH,
            ).start()
        others = buf.at[pl.ds(0, count - 1)]

        def arrived():
            pltpu.make_async_copy(others, others, rs).wait()
            total = buf[0]
            for k in range(1, count):
                total = total + buf[k]
            return total

        def sent():
            pltpu.make_async_copy(others, others, ss).wait()

        return arrived, sent

    buf1[g1] = tile
    arrived1, sent1 = exchange(buf1, n1, g1, g1_id, ss1, rs1)

    hsend_y[0] = packed_lanes(h, 0, 127)
    hsend_y[1] = packed_lanes(h, 2, 127)
    for c in range(2):
        for b in range(NV):
            for comp in (1, 2):
                hsend_x[c, b, comp - 1] = jnp.concatenate(
                    [h[c, b, comp, z, 15:16, :] for z in range(nz)], axis=0
                )
    dn_z = remote(h.at[:, :, 0:2, nz - 1], dn_zh, 3, {"gz": 1})
    dn_x = remote(hsend_x, dn_xh, 4, gx_id(gx_up))
    dn_y = remote(hsend_y, dn_yh, 5, {"gy": gy_up})

    @pl.when(gz == 0)
    def _():
        dn_z.start()

    dn_x.start()
    dn_y.start()

    pl.semaphore_wait(far, 4)
    buf2[gy] = arrived1()
    arrived2, sent2 = exchange(buf2, n_gy, gy, lambda k: {"gy": k}, ss2, rs2)

    dn_x.wait_recv()
    dn_y.wait_recv()

    @pl.when(gz == 1)
    def _():
        dn_z.wait_recv()

    @pl.when(gz == 0)
    def _():
        dn_zh[...] = jnp.zeros(dn_zh.shape, jnp.float32)

    @pl.when(gx == 0)
    def _():
        dn_xh[...] = jnp.zeros(dn_xh.shape, jnp.float32)

    @pl.when(gy == 0)
    def _():
        dn_yh[...] = jnp.zeros(dn_yh.shape, jnp.float32)

    def backward(z, behind_z):
        er, ei = eps[0, z], eps[1, z]
        for b in range(NV):
            f = [pair(h, b, comp, z) for comp in range(3)]
            dx, dy, dz = {}, {}, {}
            for comp in (1, 2):
                behind = tuple(
                    jnp.where(
                        row16 == 0,
                        dn_xh[c, b, comp - 1, pl.ds(z, 1), :],
                        pltpu.roll(f[comp][c], 1, 0),
                    )
                    for c in range(2)
                )
                dx[comp] = cmul(stretch(1), csub(f[comp], behind))
            for comp in (0, 2):
                behind = tuple(
                    jnp.where(
                        lane16 == 0,
                        unpacked(dn_yh, comp // 2, c, b, z, 128),
                        pltpu.roll(f[comp][c], 1, 1),
                    )
                    for c in range(2)
                )
                dy[comp] = cmul(stretch(4), csub(f[comp], behind))
            for comp in (0, 1):
                dz[comp] = cmul(stretch_z(1, z), csub(f[comp], behind_z(b, comp)))
            turned = curl(dx, dy, dz)
            shifted = (er + ritz[0, b], ei + ritz[1, b])
            for comp in range(3):
                out = csub(turned[comp], cmul(shifted, pair(basis, b, comp, z)))
                resid[0, b, comp, z] = out[0]
                resid[1, b, comp, z] = out[1]

    backward(0, lambda b, comp: pair(dn_zh, b, comp))

    def backward_step(z, carry):
        backward(z, lambda b, comp: pair(h, b, comp, z - 1))
        return carry

    lax.fori_loop(1, nz, backward_step, 0)

    buf3[zz] = arrived2()
    arrived3, sent3 = exchange(buf3, n_zz, zz, lambda k: {"zz": k}, ss3, rs3)

    @pl.when(gz == 1)
    def _():
        up_z.wait_send()

    @pl.when(gz == 0)
    def _():
        dn_z.wait_send()

    for copy in (up_x, up_y, dn_x, dn_y):
        copy.wait_send()
    sent1()
    sent2()
    final = arrived3() * (1.0 / (3.0 * total_x * total_y * total_z))
    gram[0] = final[0:NV, 0:NV]
    gram[1] = final[NV : 2 * NV, 0:NV]
    sent3()


def write_out(basis, resid, gram, basis_out, resid_out, gram_out, sem):
    copies = [pltpu.make_async_copy(gram, gram_out, sem.at[16])]
    for k in range(8):
        c, a = k // 4, k % 4
        copies.append(pltpu.make_async_copy(basis.at[c, a], basis_out.at[c, a], sem.at[2 * k]))
        copies.append(pltpu.make_async_copy(resid.at[c, a], resid_out.at[c, a], sem.at[2 * k + 1]))
    for copy in copies:
        copy.start()
    for copy in copies:
        copy.wait()


def body(sizes, fields, material, pml_width, eps_real, eps_loss, coeffs, ritz):
    nz, nx, ny, n_gx, n_gy, n_gz, n_zz = sizes
    n1 = n_gx // n_zz * n_gz
    whole = fields.shape
    f32 = jnp.float32
    vmem = pl.BlockSpec(memory_space=pltpu.VMEM)
    face_x = pltpu.VMEM((2, NV, 2, nz, ny), f32)
    face_y = pltpu.VMEM((2, 8, 128), f32)
    face_z = pltpu.VMEM((2, NV, 2, nx, ny), f32)
    dma = pltpu.SemaphoreType.DMA
    made = pl.pallas_call(
        functools.partial(kernel, sizes),
        out_shape=(
            jax.ShapeDtypeStruct(whole, f32),
            jax.ShapeDtypeStruct(whole, f32),
            jax.ShapeDtypeStruct((2, NV, NV), f32),
        ),
        in_specs=[pl.BlockSpec(memory_space=pltpu.HBM)] * 7,
        out_specs=(vmem, vmem, vmem),
        scratch_shapes=[
            pltpu.SMEM((6,), jnp.int32),
            pltpu.SMEM((4,), f32),
            pltpu.SMEM((4,), f32),
            pltpu.SMEM((2, NV, NV), f32),
            pltpu.SMEM((2, NV), f32),
            pltpu.VMEM((nz, nx, ny), jnp.int32),
            pltpu.VMEM(whole, f32),
            pltpu.VMEM(whole, f32),
            pltpu.VMEM((3, NV, 3, nx, ny), f32),
            pltpu.VMEM((3, NV, NV, 8, 128), f32),
            pltpu.VMEM((3, len(PAIRS), 8, 128), f32),
            pltpu.VMEM((2, nz, nx, ny), f32),
            pltpu.VMEM((6, 2, nx, ny), f32),
            pltpu.VMEM((2, 2, nz + 1, 8, 128), f32),
            face_x, face_y, face_x, face_y, face_z, face_z,
            face_x, face_y, face_x, face_y, face_z,
            pltpu.VMEM((n1, 8, 128), f32),
            pltpu.VMEM((n_gy, 8, 128), f32),
            pltpu.VMEM((n_zz, 8, 128), f32),
            dma((6,)),
            dma,
            dma((6,)),
            dma((6,)),
            dma, dma, dma, dma, dma, dma,
            pltpu.SemaphoreType.REGULAR,
            pltpu.SemaphoreType.REGULAR,
        ],
        compiler_params=pltpu.CompilerParams(
            collective_id=0, has_side_effects=True, vmem_limit_bytes=24 * 1024 * 1024
        ),
    )(*(pltpu.with_memory_space_constraint(x, pltpu.HBM) for x in (pml_width, eps_real, eps_loss, coeffs, ritz, material, fields)))
    hbm = pl.BlockSpec(memory_space=pltpu.HBM)
    return pl.pallas_call(
        write_out,
        out_shape=tuple(jax.ShapeDtypeStruct(x.shape, f32) for x in made),
        in_specs=[vmem] * 3,
        out_specs=(hbm,) * 3,
        scratch_shapes=[dma((17,))],
        compiler_params=pltpu.CompilerParams(vmem_limit_bytes=1024 * 1024),
    )(*made)


def solution(mesh):
    n_gx, n_gy, n_gz = mesh.shape["gx"], mesh.shape["gy"], mesh.shape["gz"]
    n_zz = n_gx // 4
    split = Mesh(
        mesh.devices.reshape(2, n_zz, 2, n_gy, n_gz),
        ("xh", "zz", "core", "gy", "gz"),
    )
    sizes = (16 // n_gz, 512 // n_gx, 1024 // n_gy, n_gx, n_gy, n_gz, n_zz)
    placed = (P(None, None, None, "gz", GX, "gy"), P("gz", GX, "gy"), P(), P(), P(), P(), P())
    return jax.shard_map(
        functools.partial(body, sizes),
        mesh=split,
        in_specs=placed,
        out_specs=(P(None, None, None, "gz", GX, "gy"), P(None, None, None, "gz", GX, "gy"), P()),
        check_vma=False,
    )
```

```python
import functools

import jax
import jax.numpy as jnp
from jax import lax
from jax.experimental import pallas as pl
from jax.experimental.pallas import tpu as pltpu
from jax.sharding import Mesh
from jax.sharding import PartitionSpec as P

GX = ("xh", "zz", "core")
OMEGA_SQ = 0.36
SIGMA_TOP = 3.0
NV = 4
MESH = pl.DeviceIdType.MESH
PAIRS = [(a, b) for a in range(NV) for b in range(a, NV)]


def inverse_stretch(places, length, low_width, high_width):
    inside_depth = jnp.clip((low_width - places) / low_width, 0.0, 1.0) + jnp.clip(
        (places + 1.0 - length + high_width) / high_width, 0.0, 1.0
    )
    absorb = SIGMA_TOP * inside_depth * inside_depth
    scaled = 1.0 / (1.0 + absorb * absorb)
    return scaled, -absorb * scaled


def cmul(f, v):
    return (f[0] * v[0] - f[1] * v[1], f[0] * v[1] + f[1] * v[0])


def csub(p, q):
    return (p[0] - q[0], p[1] - q[1])


def curl(dx, dy, dz):
    return (
        csub(dy[2], dz[1]),
        csub(dz[0], dx[2]),
        csub(dx[1], dy[0]),
    )


def fold(x):
    return x[0:8] + x[8:16]


def kernel(
    sizes,
    pml_hbm, eps_r_hbm, eps_l_hbm, coef_hbm, ritz_hbm, mat_hbm, fields,
    basis, resid, gram,
    pml, eps_r, eps_l, coef, ritz, mat, v, h, gs, acc, sym, eps, sxy, sz,
    send_x, send_y, up_xh, up_yh, up_raw, layers,
    hsend_x, hsend_y, dn_xh, dn_yh, dn_zh,
    buf1, buf2, buf3,
    small_sem, load_sem, halo_send, halo_recv, ss1, rs1, ss2, rs2, ss3, rs3, near, far,
):
    nz, nx, ny, n_gx, n_gy, n_gz, n_zz = sizes
    n_x = n_gx // (2 * n_zz)
    xh, zz, core = (lax.axis_index(name) for name in GX)
    gy, gz = lax.axis_index("gy"), lax.axis_index("gz")
    gx = (xh * n_zz + zz) * 2 + core
    n1 = n_x * n_gz * 2
    g1 = (xh * n_gz + gz) * 2 + core

    def gx_id(index):
        return {"xh": index // (2 * n_zz), "zz": (index // 2) % n_zz, "core": index % 2}

    def g1_id(index):
        return {"xh": index // (2 * n_gz), "gz": (index // 2) % n_gz, "core": index % 2}

    gx_up, gx_dn = (gx + 1) % n_gx, (gx + n_gx - 1) % n_gx
    gy_up, gy_dn = (gy + 1) % n_gy, (gy + n_gy - 1) % n_gy

    smalls = [
        pltpu.make_async_copy(src, dst, small_sem.at[k])
        for k, (src, dst) in enumerate(
            (
                (coef_hbm, coef), (pml_hbm, pml), (eps_r_hbm, eps_r),
                (eps_l_hbm, eps_l), (ritz_hbm, ritz), (mat_hbm, mat),
            )
        )
    ]
    for copy in smalls:
        copy.start()

    for comp in (0, 2, 1):
        for c in range(2):
            pltpu.make_async_copy(
                fields.at[c, :, comp], v.at[c, :, comp], load_sem.at[comp]
            ).start()

    barrier = pltpu.get_barrier_semaphore()

    def signal(sem, device_id):
        pl.semaphore_signal(sem, inc=1, device_id=device_id, device_id_type=MESH)

    def beside(step):
        return (
            {"gy": (gy + step) % n_gy},
            {"gy": (gy + n_gy - step) % n_gy},
            {"zz": (zz + step) % n_zz},
            {"zz": (zz + n_zz - step) % n_zz},
        )

    greeted = [gx_id(gx_up), gx_id(gx_dn)] + list(beside(1))
    greeted += [g1_id((g1 + d) % n1) for d in range(1, n1)]
    for device_id in greeted:
        signal(barrier, device_id)

    def remote(src, dst, slot, device_id):
        return pltpu.make_async_remote_copy(
            src_ref=src, dst_ref=dst, send_sem=halo_send.at[slot], recv_sem=halo_recv.at[slot],
            device_id=device_id, device_id_type=MESH,
        )

    up_z = remote(fields.at[:, :, 0:2, 0], up_raw, 0, {"gz": 0})
    up_x = remote(send_x, up_xh, 1, gx_id(gx_dn))
    up_y = remote(send_y, up_yh, 2, {"gy": gy_dn})

    pl.semaphore_wait(barrier, len(greeted))

    @pl.when(gz == 1)
    def _():
        up_z.start()
        up_raw[...] = jnp.zeros(up_raw.shape, jnp.float32)

    for copy in smalls:
        copy.wait()

    for device_id in beside(1):
        signal(near, device_id)

    row16 = lax.broadcasted_iota(jnp.int32, (16, 128), 0)
    lane16 = lax.broadcasted_iota(jnp.int32, (16, 128), 1)
    lane8 = lax.broadcasted_iota(jnp.int32, (8, 128), 1)
    row8 = lax.broadcasted_iota(jnp.int32, (8, 128), 0)

    def width(slot):
        return jnp.full((8, 128), pml[slot], jnp.int32).astype(jnp.float32)

    def put(kind, places, length, low, high):
        value = inverse_stretch(places, float(length), low, high)
        sxy[kind, 0] = value[0]
        sxy[kind, 1] = value[1]

    px = (row16 + gx * nx).astype(jnp.float32)
    py = (lane16 + gy * ny).astype(jnp.float32)
    twice = lambda t: jnp.concatenate([t, t], axis=0)
    lx, hx_w, ly, hy_w = (twice(width(slot)) for slot in range(4))
    total_x, total_y, total_z = nx * n_gx, ny * n_gy, nz * n_gz
    put(0, px + 0.5, total_x, lx, hx_w)
    put(1, px, total_x, lx, hx_w)
    put(2, px + 1.0, total_x, lx, hx_w)
    put(3, py + 0.5, total_y, ly, hy_w)
    put(4, py, total_y, ly, hy_w)
    put(5, py + 1.0, total_y, ly, hy_w)
    lz, hz_w = width(4), width(5)

    def z_stretch(z, carry):
        places = jnp.full((8, 128), z + gz * nz, jnp.int32).astype(jnp.float32)
        for kind, shift in ((0, 0.5), (1, 0.0)):
            value = inverse_stretch(places + shift, float(total_z), lz, hz_w)
            sz[kind, 0, z] = value[0]
            sz[kind, 1, z] = value[1]
        return carry

    lax.fori_loop(0, nz + 1, z_stretch, 0)

    acc[...] = jnp.zeros(acc.shape, jnp.float32)
    sym[...] = jnp.zeros(sym.shape, jnp.float32)
    zero8 = jnp.zeros((8, 128), jnp.float32)

    def loaded(comp):
        pltpu.make_async_copy(fields.at[:, :, comp], v.at[:, :, comp], load_sem.at[comp]).wait()

    def combine(vr, vi, vs, b):
        both = minus = plus = None
        for a in range(NV):
            cr, ci = coef[0, a, b], coef[1, a, b]
            p, q, r = cr * vs[a], (ci - cr) * vr[a], (cr + ci) * vi[a]
            both = p if both is None else both + p
            minus = q if minus is None else minus + q
            plus = r if plus is None else plus + r
        return both - plus, both + minus

    def combined(vr, vi):
        vs = [x + y for x, y in zip(vr, vi)]
        return [combine(vr, vi, vs, b) for b in range(NV)]

    def packed_lanes(ref, comp, lane):
        at = (lane8 + (128 - lane)) % 128

        def merge(blocks, step):
            half = len(blocks) // 2
            keep = at % (2 * step) < step
            return [
                jnp.where(keep, blocks[k], pltpu.roll(blocks[k + half], step, 1)) for k in range(half)
            ]

        groups = []
        for c in range(2):
            for a in range(NV):
                blocks = [
                    ref[c, a, comp, z, 8 * t : 8 * t + 8] for z in range(nz) for t in range(2)
                ]
                for step in (8, 4, 2, 1):
                    blocks = merge(blocks, step)
                groups += blocks
        for step in (64, 32, 16):
            groups = merge(groups, step)
        return groups[0] if lane == 0 else pltpu.roll(groups[0], 128 - lane, 1)

    lane_group = lane8 // 16
    factors = []
    for d in range(8):
        factor = None
        for out in range(8):
            src = (out - d) % 8
            a, b = src % NV, out % NV
            if out // NV == src // NV:
                value = coef[0, a, b]
            elif out // NV == 0:
                value = -coef[1, a, b]
            else:
                value = coef[1, a, b]
            factor = (
                jnp.full((8, 128), value, jnp.float32)
                if factor is None
                else jnp.where(lane_group == out, value, factor)
            )
        factors.append(factor)
    for slot, comp in ((0, 0), (1, 2)):
        loaded(comp)
        raw = packed_lanes(v, comp, 0)
        turned = factors[0] * raw
        for d in range(1, 8):
            turned = turned + factors[d] * pltpu.roll(raw, 16 * d, 1)
        send_y[slot] = turned
    up_y.start()

    loaded(1)
    for comp in (1, 2):
        rows = [
            [
                jnp.concatenate([v[c, a, comp, z, 0:1, :] for z in range(nz)], axis=0)
                for a in range(NV)
            ]
            for c in range(2)
        ]
        for b, (re, im) in enumerate(combined(*rows)):
            send_x[0, b, comp - 1] = re
            send_x[1, b, comp - 1] = im
    up_x.start()

    def rotate(z, carry):
        for comp in range(3):
            vr = [v[0, a, comp, z] for a in range(NV)]
            vi = [v[1, a, comp, z] for a in range(NV)]
            for b, (re, im) in enumerate(combined(vr, vi)):
                basis[0, b, comp, z] = re
                basis[1, b, comp, z] = im
                if comp < 2:
                    layers[0, b, comp, z] = re
                    layers[1, b, comp, z] = im
        return carry

    lax.fori_loop(0, nz, rotate, 0)

    def pair(ref, *index):
        return ref[(0,) + index], ref[(1,) + index]

    def three(value):
        return value[0], value[1], value[0] + value[1]

    def dot3(left, right):
        sums = None
        for p, q in zip(left, right):
            terms = [x * y for x, y in zip(p, q)]
            sums = terms if sums is None else [x + y for x, y in zip(sums, terms)]
        return sums

    def local_gram(z, carry):
        m = mat[z]

        def pick(table):
            low = jnp.where(m == 0, table[0], table[1])
            return OMEGA_SQ * jnp.where(m < 2, low, jnp.where(m == 2, table[2], table[3]))

        er, ei = pick(eps_r), pick(eps_l)
        eps[0, z] = er
        eps[1, z] = ei
        for a in range(NV):
            q = [three(cmul((er, ei), pair(basis, a, comp, z))) for comp in range(3)]
            for b in range(a, NV):
                k = PAIRS.index((a, b))
                for part, value in enumerate(dot3(q, [three(pair(basis, b, comp, z)) for comp in range(3)])):
                    sym[part, k] += fold(value)
        return carry

    lax.fori_loop(0, nz, local_gram, 0)

    pl.semaphore_wait(near, 4)
    for device_id in beside(2):
        signal(far, device_id)

    up_x.wait_recv()
    up_y.wait_recv()

    @pl.when(gx == n_gx - 1)
    def _():
        up_xh[...] = jnp.zeros(up_xh.shape, jnp.float32)

    @pl.when(gy == n_gy - 1)
    def _():
        up_yh[...] = jnp.zeros(up_yh.shape, jnp.float32)

    def pair_z(kind, z):
        return sz[kind, 0, z], sz[kind, 1, z]

    def stretch(kind):
        return sxy[kind, 0], sxy[kind, 1]

    def stretch_z(kind, z):
        return twice(sz[kind, 0, z]), twice(sz[kind, 1, z])

    def unpacked(ref, slot, c, b, z, lane):
        parts = []
        for t in range(2):
            place = (c * NV + b) * 16 + 2 * z + t
            parts.append(pltpu.roll(ref[slot], (lane - place) % 128, 1))
        return jnp.concatenate(parts, axis=0)

    def forward(z, t, on_x, on_y, on_z):
        half = slice(8 * t, 8 * t + 8)
        plain = not (on_x or on_y or on_z)

        def stretches(base):
            return [(sxy[base + k, 0, half], sxy[base + k, 1, half]) for k in range(3)]

        sx = stretches(0) if on_x else None
        sy = stretches(3) if on_y else None
        sz3 = [pair_z(0, z), pair_z(1, z), pair_z(1, z + 1)] if on_z else None
        for b in range(NV):
            f = [pair(basis, b, comp, z, half) for comp in range(3)]

            def both(comp, ahead, factors3):
                d = csub(ahead, f[comp])
                if factors3 is None:
                    return d, d
                sh, se, se_next = factors3
                return cmul(sh, d), csub(cmul(se_next, ahead), cmul(se, f[comp]))

            dx, dy, dz = {}, {}, {}
            for comp in (1, 2):
                ahead = []
                for c in range(2):
                    if t == 0:
                        edge = basis[c, b, comp, z, 8:9]
                    else:
                        edge = up_xh[c, b, comp - 1, pl.ds(z, 1), :]
                    ahead.append(jnp.where(row8 == 7, edge, pltpu.roll(f[comp][c], 7, 0)))
                dx[comp] = both(comp, ahead, sx)
            for comp in (0, 2):
                ahead = []
                for c in range(2):
                    place = (c * NV + b) * 16 + 2 * z + t
                    edge = pltpu.roll(up_yh[comp // 2], 127 - place, 1)
                    ahead.append(jnp.where(lane8 == 127, edge, pltpu.roll(f[comp][c], 127, 1)))
                dy[comp] = both(comp, ahead, sy)
            for comp in (0, 1):
                dz[comp] = both(comp, pair(layers, b, comp, z + 1, half), sz3)
            turned = curl(*({k: x[0] for k, x in d.items()} for d in (dx, dy, dz)))
            for comp in range(3):
                for c in range(2):
                    h[c, b, comp, z, half] = turned[comp][c]
            if not plain:
                turned = curl(*({k: x[1] for k, x in d.items()} for d in (dx, dy, dz)))
                for comp in range(3):
                    for c, value in enumerate(three(turned[comp])):
                        gs[c, b, comp] = value
        for b in range(NV):
            hb = [three(pair(h, b, comp, z, half)) for comp in range(3)]
            for a in range(b + 1 if plain else NV):
                if plain:
                    ga = [three(pair(h, a, comp, z, half)) for comp in range(3)]
                else:
                    ga = [(gs[0, a, comp], gs[1, a, comp], gs[2, a, comp]) for comp in range(3)]
                for part, value in enumerate(dot3(ga, hb)):
                    if plain:
                        sym[part, PAIRS.index((a, b))] -= value
                    else:
                        acc[part, a, b] += value

    y_edge = jnp.logical_or(gy == 0, gy == n_gy - 1)
    last = nz - 1

    def sweep(phase, carry):
        @pl.when(phase == 1)
        def _():
            @pl.when(gz == 0)
            def _():
                up_z.wait_recv()

            for comp in range(2):
                vr = [up_raw[0, a, comp] for a in range(NV)]
                vi = [up_raw[1, a, comp] for a in range(NV)]
                for b, (re, im) in enumerate(combined(vr, vi)):
                    layers[0, b, comp, nz] = re
                    layers[1, b, comp, nz] = im

        on_lo = (1 - phase) * ((nz - 5) * gz) + phase * last
        on_hi = (1 - phase) * (4 + (nz - 5) * gz) + phase * (last + gz)
        off_lo = (1 - phase) * (4 * (1 - gz)) + phase * last
        off_hi = (1 - phase) * (last - 4 * gz) + phase * (nz - gz)

        def layers_of(t, on_x, on_y):
            for on_z, lo, hi in ((True, on_lo, on_hi), (False, off_lo, off_hi)):
                def step(z, inner, on_z=on_z):
                    forward(z, t, on_x, on_y, on_z)
                    return inner

                lax.fori_loop(lo, hi, step, 0)

        for on_y in (False, True):
            @pl.when(y_edge == on_y)
            def _():
                for t in range(2):
                    x_edge = gx == (0 if t == 0 else n_gx - 1)
                    for on_x in (False, True):
                        @pl.when(x_edge == on_x)
                        def _():
                            layers_of(t, on_x, on_y)

        return carry

    lax.fori_loop(0, 2, sweep, 0)

    tile = zero8
    for b in range(NV):
        rows = zero8
        for c in range(2):
            for a in range(NV):
                k = PAIRS.index((min(a, b), max(a, b)))
                sums = [acc[part, a, b] - sym[part, k] for part in range(3)]
                s = sums[0] - sums[1] if c == 0 else sums[2] - sums[0] - sums[1]
                s = jnp.sum(s, axis=0, keepdims=True)
                rows = jnp.where(row8 == c * NV + a, s, rows)
        total = jnp.sum(rows, axis=1, keepdims=True)
        tile = jnp.where(lane8 == b, total, tile)

    def exchange(buf, count, me, ids, ss, rs):
        for d in range(1, count):
            pltpu.make_async_remote_copy(
                src_ref=buf.at[me], dst_ref=buf.at[me], send_sem=ss, recv_sem=rs,
                device_id=ids((me + d) % count), device_id_type=MESH,
            ).start()
        others = buf.at[pl.ds(0, count - 1)]

        def arrived():
            pltpu.make_async_copy(others, others, rs).wait()
            total = buf[0]
            for k in range(1, count):
                total = total + buf[k]
            return total

        def sent():
            pltpu.make_async_copy(others, others, ss).wait()

        return arrived, sent

    buf1[g1] = tile
    arrived1, sent1 = exchange(buf1, n1, g1, g1_id, ss1, rs1)

    hsend_y[0] = packed_lanes(h, 0, 127)
    hsend_y[1] = packed_lanes(h, 2, 127)
    for c in range(2):
        for b in range(NV):
            for comp in (1, 2):
                hsend_x[c, b, comp - 1] = jnp.concatenate(
                    [h[c, b, comp, z, 15:16, :] for z in range(nz)], axis=0
                )
    dn_z = remote(h.at[:, :, 0:2, nz - 1], dn_zh, 3, {"gz": 1})
    dn_x = remote(hsend_x, dn_xh, 4, gx_id(gx_up))
    dn_y = remote(hsend_y, dn_yh, 5, {"gy": gy_up})

    @pl.when(gz == 0)
    def _():
        dn_z.start()

    dn_x.start()
    dn_y.start()

    pl.semaphore_wait(far, 4)
    buf2[gy] = arrived1()
    arrived2, sent2 = exchange(buf2, n_gy, gy, lambda k: {"gy": k}, ss2, rs2)

    dn_x.wait_recv()
    dn_y.wait_recv()

    @pl.when(gz == 1)
    def _():
        dn_z.wait_recv()

    @pl.when(gz == 0)
    def _():
        dn_zh[...] = jnp.zeros(dn_zh.shape, jnp.float32)

    @pl.when(gx == 0)
    def _():
        dn_xh[...] = jnp.zeros(dn_xh.shape, jnp.float32)

    @pl.when(gy == 0)
    def _():
        dn_yh[...] = jnp.zeros(dn_yh.shape, jnp.float32)

    def backward(z, behind_z):
        er, ei = eps[0, z], eps[1, z]
        for b in range(NV):
            f = [pair(h, b, comp, z) for comp in range(3)]
            dx, dy, dz = {}, {}, {}
            for comp in (1, 2):
                behind = tuple(
                    jnp.where(
                        row16 == 0,
                        dn_xh[c, b, comp - 1, pl.ds(z, 1), :],
                        pltpu.roll(f[comp][c], 1, 0),
                    )
                    for c in range(2)
                )
                dx[comp] = cmul(stretch(1), csub(f[comp], behind))
            for comp in (0, 2):
                behind = tuple(
                    jnp.where(
                        lane16 == 0,
                        unpacked(dn_yh, comp // 2, c, b, z, 128),
                        pltpu.roll(f[comp][c], 1, 1),
                    )
                    for c in range(2)
                )
                dy[comp] = cmul(stretch(4), csub(f[comp], behind))
            for comp in (0, 1):
                dz[comp] = cmul(stretch_z(1, z), csub(f[comp], behind_z(b, comp)))
            turned = curl(dx, dy, dz)
            shifted = (er + ritz[0, b], ei + ritz[1, b])
            for comp in range(3):
                out = csub(turned[comp], cmul(shifted, pair(basis, b, comp, z)))
                resid[0, b, comp, z] = out[0]
                resid[1, b, comp, z] = out[1]

    backward(0, lambda b, comp: pair(dn_zh, b, comp))

    def backward_step(z, carry):
        backward(z, lambda b, comp: pair(h, b, comp, z - 1))
        return carry

    lax.fori_loop(1, nz, backward_step, 0)

    buf3[zz] = arrived2()
    arrived3, sent3 = exchange(buf3, n_zz, zz, lambda k: {"zz": k}, ss3, rs3)

    @pl.when(gz == 1)
    def _():
        up_z.wait_send()

    @pl.when(gz == 0)
    def _():
        dn_z.wait_send()

    for copy in (up_x, up_y, dn_x, dn_y):
        copy.wait_send()
    sent1()
    sent2()
    final = arrived3() * (1.0 / (3.0 * total_x * total_y * total_z))
    gram[0] = final[0:NV, 0:NV]
    gram[1] = final[NV : 2 * NV, 0:NV]
    sent3()


def write_out(basis, resid, gram, basis_out, resid_out, gram_out, sem):
    copies = [pltpu.make_async_copy(gram, gram_out, sem.at[16])]
    for k in range(8):
        c, a = k // 4, k % 4
        copies.append(pltpu.make_async_copy(basis.at[c, a], basis_out.at[c, a], sem.at[2 * k]))
        copies.append(pltpu.make_async_copy(resid.at[c, a], resid_out.at[c, a], sem.at[2 * k + 1]))
    for copy in copies:
        copy.start()
    for copy in copies:
        copy.wait()


def body(sizes, fields, material, pml_width, eps_real, eps_loss, coeffs, ritz):
    nz, nx, ny, n_gx, n_gy, n_gz, n_zz = sizes
    n1 = n_gx // n_zz * n_gz
    whole = fields.shape
    f32 = jnp.float32
    vmem = pl.BlockSpec(memory_space=pltpu.VMEM)
    face_x = pltpu.VMEM((2, NV, 2, nz, ny), f32)
    face_y = pltpu.VMEM((2, 8, 128), f32)
    face_z = pltpu.VMEM((2, NV, 2, nx, ny), f32)
    dma = pltpu.SemaphoreType.DMA
    made = pl.pallas_call(
        functools.partial(kernel, sizes),
        out_shape=(
            jax.ShapeDtypeStruct(whole, f32),
            jax.ShapeDtypeStruct(whole, f32),
            jax.ShapeDtypeStruct((2, NV, NV), f32),
        ),
        in_specs=[pl.BlockSpec(memory_space=pltpu.HBM)] * 7,
        out_specs=(vmem, vmem, vmem),
        scratch_shapes=[
            pltpu.SMEM((6,), jnp.int32),
            pltpu.SMEM((4,), f32),
            pltpu.SMEM((4,), f32),
            pltpu.SMEM((2, NV, NV), f32),
            pltpu.SMEM((2, NV), f32),
            pltpu.VMEM((nz, nx, ny), jnp.int32),
            pltpu.VMEM(whole, f32),
            pltpu.VMEM(whole, f32),
            pltpu.VMEM((3, NV, 3, 8, 128), f32),
            pltpu.VMEM((3, NV, NV, 8, 128), f32),
            pltpu.VMEM((3, len(PAIRS), 8, 128), f32),
            pltpu.VMEM((2, nz, nx, ny), f32),
            pltpu.VMEM((6, 2, nx, ny), f32),
            pltpu.VMEM((2, 2, nz + 1, 8, 128), f32),
            face_x, face_y, face_x, face_y, face_z,
            pltpu.VMEM((2, NV, 2, nz + 1, nx, ny), f32),
            face_x, face_y, face_x, face_y, face_z,
            pltpu.VMEM((n1, 8, 128), f32),
            pltpu.VMEM((n_gy, 8, 128), f32),
            pltpu.VMEM((n_zz, 8, 128), f32),
            dma((6,)),
            dma((3,)),
            dma((6,)),
            dma((6,)),
            dma, dma, dma, dma, dma, dma,
            pltpu.SemaphoreType.REGULAR,
            pltpu.SemaphoreType.REGULAR,
        ],
        compiler_params=pltpu.CompilerParams(
            collective_id=0, has_side_effects=True, vmem_limit_bytes=24 * 1024 * 1024
        ),
    )(*(pltpu.with_memory_space_constraint(x, pltpu.HBM) for x in (pml_width, eps_real, eps_loss, coeffs, ritz, material, fields)))
    hbm = pl.BlockSpec(memory_space=pltpu.HBM)
    return pl.pallas_call(
        write_out,
        out_shape=tuple(jax.ShapeDtypeStruct(x.shape, f32) for x in made),
        in_specs=[vmem] * 3,
        out_specs=(hbm,) * 3,
        scratch_shapes=[dma((17,))],
        compiler_params=pltpu.CompilerParams(vmem_limit_bytes=1024 * 1024),
    )(*made)


def solution(mesh):
    n_gx, n_gy, n_gz = mesh.shape["gx"], mesh.shape["gy"], mesh.shape["gz"]
    n_zz = n_gx // 4
    split = Mesh(
        mesh.devices.reshape(2, n_zz, 2, n_gy, n_gz),
        ("xh", "zz", "core", "gy", "gz"),
    )
    sizes = (16 // n_gz, 512 // n_gx, 1024 // n_gy, n_gx, n_gy, n_gz, n_zz)
    placed = (P(None, None, None, "gz", GX, "gy"), P("gz", GX, "gy"), P(), P(), P(), P(), P())
    return jax.shard_map(
        functools.partial(body, sizes),
        mesh=split,
        in_specs=placed,
        out_specs=(P(None, None, None, "gz", GX, "gy"), P(None, None, None, "gz", GX, "gy"), P()),
        check_vma=False,
    )
```

```python
import functools

import jax
import jax.numpy as jnp
from jax import lax
from jax.experimental import pallas as pl
from jax.experimental.pallas import tpu as pltpu
from jax.sharding import Mesh
from jax.sharding import PartitionSpec as P

GX = ("xh", "zz", "core")
OMEGA_SQ = 0.36
SIGMA_TOP = 3.0
NV = 4
MESH = pl.DeviceIdType.MESH
PAIRS = [(a, b) for a in range(NV) for b in range(a, NV)]


def inverse_stretch(places, length, low_width, high_width):
    inside_depth = jnp.clip((low_width - places) / low_width, 0.0, 1.0) + jnp.clip(
        (places + 1.0 - length + high_width) / high_width, 0.0, 1.0
    )
    absorb = SIGMA_TOP * inside_depth * inside_depth
    scaled = 1.0 / (1.0 + absorb * absorb)
    return scaled, -absorb * scaled


def cmul(f, v):
    return (f[0] * v[0] - f[1] * v[1], f[0] * v[1] + f[1] * v[0])


def csub(p, q):
    return (p[0] - q[0], p[1] - q[1])


def curl(dx, dy, dz):
    return (
        csub(dy[2], dz[1]),
        csub(dz[0], dx[2]),
        csub(dx[1], dy[0]),
    )


def fold(x):
    return x[0:8] + x[8:16]


def kernel(
    sizes,
    pml_hbm, eps_r_hbm, eps_l_hbm, coef_hbm, ritz_hbm, mat_hbm, fields,
    basis, resid, gram,
    pml, eps_r, eps_l, coef, ritz, mat, v, h, gs, acc, sym, eps, sxy, sz,
    send_x, send_y, up_xh, up_yh, up_raw, layers,
    hsend_x, hsend_y, dn_xh, dn_yh, dn_zh,
    buf1, buf2, buf3,
    small_sem, load_sem, halo_send, halo_recv, ss1, rs1, ss2, rs2, ss3, rs3, near, far,
):
    nz, nx, ny, n_gx, n_gy, n_gz, n_zz = sizes
    n_x = n_gx // (2 * n_zz)
    xh, zz, core = (lax.axis_index(name) for name in GX)
    gy, gz = lax.axis_index("gy"), lax.axis_index("gz")
    gx = (xh * n_zz + zz) * 2 + core
    n1 = n_x * n_gz * 2
    g1 = (xh * n_gz + gz) * 2 + core

    def gx_id(index):
        return {"xh": index // (2 * n_zz), "zz": (index // 2) % n_zz, "core": index % 2}

    def g1_id(index):
        return {"xh": index // (2 * n_gz), "gz": (index // 2) % n_gz, "core": index % 2}

    gx_up, gx_dn = (gx + 1) % n_gx, (gx + n_gx - 1) % n_gx
    gy_up, gy_dn = (gy + 1) % n_gy, (gy + n_gy - 1) % n_gy

    smalls = [
        pltpu.make_async_copy(src, dst, small_sem.at[k])
        for k, (src, dst) in enumerate(
            (
                (coef_hbm, coef), (pml_hbm, pml), (eps_r_hbm, eps_r),
                (eps_l_hbm, eps_l), (ritz_hbm, ritz), (mat_hbm, mat),
            )
        )
    ]
    for copy in smalls:
        copy.start()

    for comp in (0, 2, 1):
        for c in range(2):
            pltpu.make_async_copy(
                fields.at[c, :, comp], v.at[c, :, comp], load_sem.at[comp]
            ).start()

    barrier = pltpu.get_barrier_semaphore()

    def signal(sem, device_id):
        pl.semaphore_signal(sem, inc=1, device_id=device_id, device_id_type=MESH)

    def beside(step):
        return (
            {"gy": (gy + step) % n_gy},
            {"gy": (gy + n_gy - step) % n_gy},
            {"zz": (zz + step) % n_zz},
            {"zz": (zz + n_zz - step) % n_zz},
        )

    greeted = [gx_id(gx_up), gx_id(gx_dn)] + list(beside(1))
    greeted += [g1_id((g1 + d) % n1) for d in range(1, n1)]
    for device_id in greeted:
        signal(barrier, device_id)

    def remote(src, dst, slot, device_id):
        return pltpu.make_async_remote_copy(
            src_ref=src, dst_ref=dst, send_sem=halo_send.at[slot], recv_sem=halo_recv.at[slot],
            device_id=device_id, device_id_type=MESH,
        )

    up_z = remote(fields.at[:, :, 0:2, 0], up_raw, 0, {"gz": 0})
    up_x = remote(send_x, up_xh, 1, gx_id(gx_dn))
    up_y = remote(send_y, up_yh, 2, {"gy": gy_dn})

    pl.semaphore_wait(barrier, len(greeted))

    @pl.when(gz == 1)
    def _():
        up_z.start()
        up_raw[...] = jnp.zeros(up_raw.shape, jnp.float32)

    for copy in smalls:
        copy.wait()

    for device_id in beside(1):
        signal(near, device_id)

    row16 = lax.broadcasted_iota(jnp.int32, (16, 128), 0)
    lane16 = lax.broadcasted_iota(jnp.int32, (16, 128), 1)
    lane8 = lax.broadcasted_iota(jnp.int32, (8, 128), 1)
    row8 = lax.broadcasted_iota(jnp.int32, (8, 128), 0)

    def width(slot):
        return jnp.full((8, 128), pml[slot], jnp.int32).astype(jnp.float32)

    def put(kind, places, length, low, high):
        value = inverse_stretch(places, float(length), low, high)
        sxy[kind, 0] = value[0]
        sxy[kind, 1] = value[1]

    px = (row16 + gx * nx).astype(jnp.float32)
    py = (lane16 + gy * ny).astype(jnp.float32)
    twice = lambda t: jnp.concatenate([t, t], axis=0)
    lx, hx_w, ly, hy_w = (twice(width(slot)) for slot in range(4))
    total_x, total_y, total_z = nx * n_gx, ny * n_gy, nz * n_gz
    put(0, px + 0.5, total_x, lx, hx_w)
    put(1, px, total_x, lx, hx_w)
    put(2, px + 1.0, total_x, lx, hx_w)
    put(3, py + 0.5, total_y, ly, hy_w)
    put(4, py, total_y, ly, hy_w)
    put(5, py + 1.0, total_y, ly, hy_w)
    lz, hz_w = width(4), width(5)

    def z_stretch(z, carry):
        places = jnp.full((8, 128), z + gz * nz, jnp.int32).astype(jnp.float32)
        for kind, shift in ((0, 0.5), (1, 0.0)):
            value = inverse_stretch(places + shift, float(total_z), lz, hz_w)
            sz[kind, 0, z] = value[0]
            sz[kind, 1, z] = value[1]
        return carry

    lax.fori_loop(0, nz + 1, z_stretch, 0)

    acc[...] = jnp.zeros(acc.shape, jnp.float32)
    sym[...] = jnp.zeros(sym.shape, jnp.float32)
    zero8 = jnp.zeros((8, 128), jnp.float32)

    def loaded(comp):
        pltpu.make_async_copy(fields.at[:, :, comp], v.at[:, :, comp], load_sem.at[comp]).wait()

    def combine(vr, vi, vs, b):
        both = minus = plus = None
        for a in range(NV):
            cr, ci = coef[0, a, b], coef[1, a, b]
            p, q, r = cr * vs[a], (ci - cr) * vr[a], (cr + ci) * vi[a]
            both = p if both is None else both + p
            minus = q if minus is None else minus + q
            plus = r if plus is None else plus + r
        return both - plus, both + minus

    def combined(vr, vi):
        vs = [x + y for x, y in zip(vr, vi)]
        return [combine(vr, vi, vs, b) for b in range(NV)]

    def packed_lanes(ref, comp, lane):
        tile = None
        for c in range(2):
            for a in range(NV):
                part = None
                for z in range(nz):
                    for t in range(2):
                        column = ref[c, a, comp, z, 8 * t : 8 * t + 8, lane : lane + 1]
                        column = jnp.broadcast_to(column, (8, 128))
                        place = 2 * z + t
                        part = column if part is None else jnp.where(lane_in == place, column, part)
                group = c * NV + a
                tile = part if tile is None else jnp.where(lane_group == group, part, tile)
        return tile

    lane_in, lane_group = lane8 % 16, lane8 // 16
    factors = []
    for d in range(8):
        factor = None
        for out in range(8):
            src = (out - d) % 8
            a, b = src % NV, out % NV
            if out // NV == src // NV:
                value = coef[0, a, b]
            elif out // NV == 0:
                value = -coef[1, a, b]
            else:
                value = coef[1, a, b]
            factor = (
                jnp.full((8, 128), value, jnp.float32)
                if factor is None
                else jnp.where(lane_group == out, value, factor)
            )
        factors.append(factor)
    for slot, comp in ((0, 0), (1, 2)):
        loaded(comp)
        raw = packed_lanes(v, comp, 0)
        turned = factors[0] * raw
        for d in range(1, 8):
            turned = turned + factors[d] * pltpu.roll(raw, 16 * d, 1)
        send_y[slot] = turned
    up_y.start()

    loaded(1)
    for comp in (1, 2):
        rows = [
            [
                jnp.concatenate([v[c, a, comp, z, 0:1, :] for z in range(nz)], axis=0)
                for a in range(NV)
            ]
            for c in range(2)
        ]
        for b, (re, im) in enumerate(combined(*rows)):
            send_x[0, b, comp - 1] = re
            send_x[1, b, comp - 1] = im
    up_x.start()

    def rotate(z, carry):
        for comp in range(3):
            vr = [v[0, a, comp, z] for a in range(NV)]
            vi = [v[1, a, comp, z] for a in range(NV)]
            for b, (re, im) in enumerate(combined(vr, vi)):
                basis[0, b, comp, z] = re
                basis[1, b, comp, z] = im
                if comp < 2:
                    layers[0, b, comp, z] = re
                    layers[1, b, comp, z] = im
        return carry

    lax.fori_loop(0, nz, rotate, 0)

    def pair(ref, *index):
        return ref[(0,) + index], ref[(1,) + index]

    def three(value):
        return value[0], value[1], value[0] + value[1]

    def dot3(left, right):
        sums = None
        for p, q in zip(left, right):
            terms = [x * y for x, y in zip(p, q)]
            sums = terms if sums is None else [x + y for x, y in zip(sums, terms)]
        return sums

    def local_gram(z, carry):
        m = mat[z]

        def pick(table):
            low = jnp.where(m == 0, table[0], table[1])
            return OMEGA_SQ * jnp.where(m < 2, low, jnp.where(m == 2, table[2], table[3]))

        er, ei = pick(eps_r), pick(eps_l)
        eps[0, z] = er
        eps[1, z] = ei
        for a in range(NV):
            q = [three(cmul((er, ei), pair(basis, a, comp, z))) for comp in range(3)]
            for b in range(a, NV):
                k = PAIRS.index((a, b))
                for part, value in enumerate(dot3(q, [three(pair(basis, b, comp, z)) for comp in range(3)])):
                    sym[part, k] += fold(value)
        return carry

    lax.fori_loop(0, nz, local_gram, 0)

    pl.semaphore_wait(near, 4)
    for device_id in beside(2):
        signal(far, device_id)

    up_x.wait_recv()
    up_y.wait_recv()

    @pl.when(gx == n_gx - 1)
    def _():
        up_xh[...] = jnp.zeros(up_xh.shape, jnp.float32)

    @pl.when(gy == n_gy - 1)
    def _():
        up_yh[...] = jnp.zeros(up_yh.shape, jnp.float32)

    def stretch(kind):
        return sxy[kind, 0], sxy[kind, 1]

    def stretch_z(kind, z):
        return twice(sz[kind, 0, z]), twice(sz[kind, 1, z])

    def unpacked(ref, slot, c, b, z, lane):
        parts = []
        for t in range(2):
            place = (c * NV + b) * 16 + 2 * z + t
            parts.append(pltpu.roll(ref[slot], (lane - place) % 128, 1))
        return jnp.concatenate(parts, axis=0)

    def forward(z, on_x, on_y, on_z):
        plain = not (on_x or on_y or on_z)
        sx = [stretch(k) for k in range(3)] if on_x else None
        sy = [stretch(3 + k) for k in range(3)] if on_y else None
        sz3 = [stretch_z(0, z), stretch_z(1, z), stretch_z(1, z + 1)] if on_z else None
        for b in range(NV):
            f = [pair(basis, b, comp, z) for comp in range(3)]

            def both(comp, ahead, factors3, upper=False):
                d = csub(ahead, f[comp])
                if factors3 is None:
                    return d, d
                rows = slice(8, 16) if upper else slice(0, 16)
                part = lambda value: [x[rows] for x in value]
                sh, se, se_next = (part(x) for x in factors3)
                near_part, far_part = part(f[comp]), part(ahead)
                results = cmul(sh, part(d)), csub(cmul(se_next, far_part), cmul(se, near_part))
                if not upper:
                    return results
                return tuple(
                    [jnp.concatenate([d[c][0:8], value[c]], axis=0) for c in range(2)]
                    for value in results
                )

            dx, dy, dz = {}, {}, {}
            for comp in (1, 2):
                ahead = [
                    jnp.where(
                        row16 == 15,
                        up_xh[c, b, comp - 1, pl.ds(z, 1), :],
                        pltpu.roll(f[comp][c], 15, 0),
                    )
                    for c in range(2)
                ]
                dx[comp] = both(comp, ahead, sx, on_x == "upper")
            for comp in (0, 2):
                ahead = [
                    jnp.where(
                        lane16 == 127,
                        unpacked(up_yh, comp // 2, c, b, z, 127),
                        pltpu.roll(f[comp][c], 127, 1),
                    )
                    for c in range(2)
                ]
                dy[comp] = both(comp, ahead, sy)
            for comp in (0, 1):
                dz[comp] = both(comp, pair(layers, b, comp, z + 1), sz3)
            turned = curl(*({k: x[0] for k, x in d.items()} for d in (dx, dy, dz)))
            for comp in range(3):
                for c in range(2):
                    h[c, b, comp, z] = turned[comp][c]
            if not plain:
                turned = curl(*({k: x[1] for k, x in d.items()} for d in (dx, dy, dz)))
                for comp in range(3):
                    for c, value in enumerate(three(turned[comp])):
                        gs[c, b, comp] = value
        for b in range(NV):
            hb = [three(pair(h, b, comp, z)) for comp in range(3)]
            for a in range(b + 1 if plain else NV):
                if plain:
                    ga = [three(pair(h, a, comp, z)) for comp in range(3)]
                else:
                    ga = [(gs[0, a, comp], gs[1, a, comp], gs[2, a, comp]) for comp in range(3)]
                for part, value in enumerate(dot3(ga, hb)):
                    if plain:
                        sym[part, PAIRS.index((a, b))] -= fold(value)
                    else:
                        acc[part, a, b] += fold(value)

    edge = jnp.logical_or(jnp.logical_or(gy == 0, gy == n_gy - 1), gx == 0)
    x_end = gx == n_gx - 1
    last = nz - 1

    def sweep(phase, carry):
        @pl.when(phase == 1)
        def _():
            @pl.when(gz == 0)
            def _():
                up_z.wait_recv()

            for comp in range(2):
                vr = [up_raw[0, a, comp] for a in range(NV)]
                vi = [up_raw[1, a, comp] for a in range(NV)]
                for b, (re, im) in enumerate(combined(vr, vi)):
                    layers[0, b, comp, nz] = re
                    layers[1, b, comp, nz] = im

        on_lo = (1 - phase) * ((nz - 5) * gz) + phase * last
        on_hi = (1 - phase) * (4 + (nz - 5) * gz) + phase * (last + gz)
        off_lo = (1 - phase) * (4 * (1 - gz)) + phase * last
        off_hi = (1 - phase) * (last - 4 * gz) + phase * (nz - gz)

        def run(lo, hi, *flags):
            def step(z, inner):
                forward(z, *flags)
                return inner

            lax.fori_loop(lo, hi, step, 0)

        @pl.when(edge)
        def _():
            run(phase * last, last + phase, "all", True, True)

        @pl.when(jnp.logical_not(edge))
        def _():
            for at_end, on_x in ((False, None), (True, "upper")):
                @pl.when(x_end == at_end)
                def _():
                    run(on_lo, on_hi, on_x, False, True)
                    run(off_lo, off_hi, on_x, False, False)

        return carry

    lax.fori_loop(0, 2, sweep, 0)

    tile = zero8
    for b in range(NV):
        rows = zero8
        for c in range(2):
            for a in range(NV):
                k = PAIRS.index((min(a, b), max(a, b)))
                sums = [acc[part, a, b] - sym[part, k] for part in range(3)]
                s = sums[0] - sums[1] if c == 0 else sums[2] - sums[0] - sums[1]
                s = jnp.sum(s, axis=0, keepdims=True)
                rows = jnp.where(row8 == c * NV + a, s, rows)
        total = jnp.sum(rows, axis=1, keepdims=True)
        tile = jnp.where(lane8 == b, total, tile)

    def exchange(buf, count, me, ids, ss, rs):
        for d in range(1, count):
            pltpu.make_async_remote_copy(
                src_ref=buf.at[me], dst_ref=buf.at[me], send_sem=ss, recv_sem=rs,
                device_id=ids((me + d) % count), device_id_type=MESH,
            ).start()
        others = buf.at[pl.ds(0, count - 1)]

        def arrived():
            pltpu.make_async_copy(others, others, rs).wait()
            total = buf[0]
            for k in range(1, count):
                total = total + buf[k]
            return total

        def sent():
            pltpu.make_async_copy(others, others, ss).wait()

        return arrived, sent

    buf1[g1] = tile
    arrived1, sent1 = exchange(buf1, n1, g1, g1_id, ss1, rs1)

    hsend_y[0] = packed_lanes(h, 0, 127)
    hsend_y[1] = packed_lanes(h, 2, 127)
    for c in range(2):
        for b in range(NV):
            for comp in (1, 2):
                hsend_x[c, b, comp - 1] = jnp.concatenate(
                    [h[c, b, comp, z, 15:16, :] for z in range(nz)], axis=0
                )
    dn_z = remote(h.at[:, :, 0:2, nz - 1], dn_zh, 3, {"gz": 1})
    dn_x = remote(hsend_x, dn_xh, 4, gx_id(gx_up))
    dn_y = remote(hsend_y, dn_yh, 5, {"gy": gy_up})

    @pl.when(gz == 0)
    def _():
        dn_z.start()

    dn_x.start()
    dn_y.start()

    pl.semaphore_wait(far, 4)
    buf2[gy] = arrived1()
    arrived2, sent2 = exchange(buf2, n_gy, gy, lambda k: {"gy": k}, ss2, rs2)

    dn_x.wait_recv()
    dn_y.wait_recv()

    @pl.when(gz == 1)
    def _():
        dn_z.wait_recv()

    @pl.when(gz == 0)
    def _():
        dn_zh[...] = jnp.zeros(dn_zh.shape, jnp.float32)

    @pl.when(gx == 0)
    def _():
        dn_xh[...] = jnp.zeros(dn_xh.shape, jnp.float32)

    @pl.when(gy == 0)
    def _():
        dn_yh[...] = jnp.zeros(dn_yh.shape, jnp.float32)

    def backward(z, behind_z):
        er, ei = eps[0, z], eps[1, z]
        for b in range(NV):
            f = [pair(h, b, comp, z) for comp in range(3)]
            dx, dy, dz = {}, {}, {}
            for comp in (1, 2):
                behind = tuple(
                    jnp.where(
                        row16 == 0,
                        dn_xh[c, b, comp - 1, pl.ds(z, 1), :],
                        pltpu.roll(f[comp][c], 1, 0),
                    )
                    for c in range(2)
                )
                dx[comp] = cmul(stretch(1), csub(f[comp], behind))
            for comp in (0, 2):
                behind = tuple(
                    jnp.where(
                        lane16 == 0,
                        unpacked(dn_yh, comp // 2, c, b, z, 128),
                        pltpu.roll(f[comp][c], 1, 1),
                    )
                    for c in range(2)
                )
                dy[comp] = cmul(stretch(4), csub(f[comp], behind))
            for comp in (0, 1):
                dz[comp] = cmul(stretch_z(1, z), csub(f[comp], behind_z(b, comp)))
            turned = curl(dx, dy, dz)
            shifted = (er + ritz[0, b], ei + ritz[1, b])
            for comp in range(3):
                out = csub(turned[comp], cmul(shifted, pair(basis, b, comp, z)))
                resid[0, b, comp, z] = out[0]
                resid[1, b, comp, z] = out[1]

    backward(0, lambda b, comp: pair(dn_zh, b, comp))

    def backward_step(z, carry):
        backward(z, lambda b, comp: pair(h, b, comp, z - 1))
        return carry

    lax.fori_loop(1, nz, backward_step, 0)

    buf3[zz] = arrived2()
    arrived3, sent3 = exchange(buf3, n_zz, zz, lambda k: {"zz": k}, ss3, rs3)

    @pl.when(gz == 1)
    def _():
        up_z.wait_send()

    @pl.when(gz == 0)
    def _():
        dn_z.wait_send()

    for copy in (up_x, up_y, dn_x, dn_y):
        copy.wait_send()
    sent1()
    sent2()
    final = arrived3() * (1.0 / (3.0 * total_x * total_y * total_z))
    gram[0] = final[0:NV, 0:NV]
    gram[1] = final[NV : 2 * NV, 0:NV]
    sent3()


def write_out(basis, resid, gram, basis_out, resid_out, gram_out, sem):
    copies = [pltpu.make_async_copy(gram, gram_out, sem.at[16])]
    for k in range(8):
        c, a = k // 4, k % 4
        copies.append(pltpu.make_async_copy(basis.at[c, a], basis_out.at[c, a], sem.at[2 * k]))
        copies.append(pltpu.make_async_copy(resid.at[c, a], resid_out.at[c, a], sem.at[2 * k + 1]))
    for copy in copies:
        copy.start()
    for copy in copies:
        copy.wait()


def body(sizes, fields, material, pml_width, eps_real, eps_loss, coeffs, ritz):
    nz, nx, ny, n_gx, n_gy, n_gz, n_zz = sizes
    n1 = n_gx // n_zz * n_gz
    whole = fields.shape
    f32 = jnp.float32
    vmem = pl.BlockSpec(memory_space=pltpu.VMEM)
    face_x = pltpu.VMEM((2, NV, 2, nz, ny), f32)
    face_y = pltpu.VMEM((2, 8, 128), f32)
    face_z = pltpu.VMEM((2, NV, 2, nx, ny), f32)
    dma = pltpu.SemaphoreType.DMA
    made = pl.pallas_call(
        functools.partial(kernel, sizes),
        out_shape=(
            jax.ShapeDtypeStruct(whole, f32),
            jax.ShapeDtypeStruct(whole, f32),
            jax.ShapeDtypeStruct((2, NV, NV), f32),
        ),
        in_specs=[pl.BlockSpec(memory_space=pltpu.HBM)] * 7,
        out_specs=(vmem, vmem, vmem),
        scratch_shapes=[
            pltpu.SMEM((6,), jnp.int32),
            pltpu.SMEM((4,), f32),
            pltpu.SMEM((4,), f32),
            pltpu.SMEM((2, NV, NV), f32),
            pltpu.SMEM((2, NV), f32),
            pltpu.VMEM((nz, nx, ny), jnp.int32),
            pltpu.VMEM(whole, f32),
            pltpu.VMEM(whole, f32),
            pltpu.VMEM((3, NV, 3, nx, ny), f32),
            pltpu.VMEM((3, NV, NV, 8, 128), f32),
            pltpu.VMEM((3, len(PAIRS), 8, 128), f32),
            pltpu.VMEM((2, nz, nx, ny), f32),
            pltpu.VMEM((6, 2, nx, ny), f32),
            pltpu.VMEM((2, 2, nz + 1, 8, 128), f32),
            face_x, face_y, face_x, face_y, face_z,
            pltpu.VMEM((2, NV, 2, nz + 1, nx, ny), f32),
            face_x, face_y, face_x, face_y, face_z,
            pltpu.VMEM((n1, 8, 128), f32),
            pltpu.VMEM((n_gy, 8, 128), f32),
            pltpu.VMEM((n_zz, 8, 128), f32),
            dma((6,)),
            dma((3,)),
            dma((6,)),
            dma((6,)),
            dma, dma, dma, dma, dma, dma,
            pltpu.SemaphoreType.REGULAR,
            pltpu.SemaphoreType.REGULAR,
        ],
        compiler_params=pltpu.CompilerParams(
            collective_id=0, has_side_effects=True, vmem_limit_bytes=24 * 1024 * 1024
        ),
    )(*(pltpu.with_memory_space_constraint(x, pltpu.HBM) for x in (pml_width, eps_real, eps_loss, coeffs, ritz, material, fields)))
    hbm = pl.BlockSpec(memory_space=pltpu.HBM)
    return pl.pallas_call(
        write_out,
        out_shape=tuple(jax.ShapeDtypeStruct(x.shape, f32) for x in made),
        in_specs=[vmem] * 3,
        out_specs=(hbm,) * 3,
        scratch_shapes=[dma((17,))],
        compiler_params=pltpu.CompilerParams(vmem_limit_bytes=1024 * 1024),
    )(*made)


def solution(mesh):
    n_gx, n_gy, n_gz = mesh.shape["gx"], mesh.shape["gy"], mesh.shape["gz"]
    n_zz = n_gx // 4
    split = Mesh(
        mesh.devices.reshape(2, n_zz, 2, n_gy, n_gz),
        ("xh", "zz", "core", "gy", "gz"),
    )
    sizes = (16 // n_gz, 512 // n_gx, 1024 // n_gy, n_gx, n_gy, n_gz, n_zz)
    placed = (P(None, None, None, "gz", GX, "gy"), P("gz", GX, "gy"), P(), P(), P(), P(), P())
    return jax.shard_map(
        functools.partial(body, sizes),
        mesh=split,
        in_specs=placed,
        out_specs=(P(None, None, None, "gz", GX, "gy"), P(None, None, None, "gz", GX, "gy"), P()),
        check_vma=False,
    )
```

```python
import functools

import jax
import jax.numpy as jnp
from jax import lax
from jax.experimental import pallas as pl
from jax.experimental.pallas import tpu as pltpu
from jax.sharding import Mesh
from jax.sharding import PartitionSpec as P

GX = ("xh", "zz", "core")
OMEGA_SQ = 0.36
SIGMA_TOP = 3.0
NV = 4
MESH = pl.DeviceIdType.MESH
PAIRS = [(a, b) for a in range(NV) for b in range(a, NV)]


def inverse_stretch(places, length, low_width, high_width):
    inside_depth = jnp.clip((low_width - places) / low_width, 0.0, 1.0) + jnp.clip(
        (places + 1.0 - length + high_width) / high_width, 0.0, 1.0
    )
    absorb = SIGMA_TOP * inside_depth * inside_depth
    scaled = 1.0 / (1.0 + absorb * absorb)
    return scaled, -absorb * scaled


def cmul(f, v):
    return (f[0] * v[0] - f[1] * v[1], f[0] * v[1] + f[1] * v[0])


def csub(p, q):
    return (p[0] - q[0], p[1] - q[1])


def curl(dx, dy, dz):
    return (
        csub(dy[2], dz[1]),
        csub(dz[0], dx[2]),
        csub(dx[1], dy[0]),
    )


def fold(x):
    return x[0:8] + x[8:16]


def kernel(
    sizes,
    pml_hbm, eps_r_hbm, eps_l_hbm, coef_hbm, ritz_hbm, mat_hbm, fields,
    basis, resid, gram,
    pml, eps_r, eps_l, coef, ritz, mat, v, h, gs, acc, sym, eps, sxy, sz,
    send_x, send_y, up_xh, up_yh, up_raw, layers,
    hsend_x, hsend_y, dn_xh, dn_yh, dn_zh,
    buf1, buf2,
    small_sem, load_sem, halo_send, halo_recv, ss1, rs1, ss2, rs2, near, far, opposite,
):
    nz, nx, ny, n_gx, n_gy, n_gz, n_zz = sizes
    n_x = n_gx // (2 * n_zz)
    xh, zz, core = (lax.axis_index(name) for name in GX)
    gy, gz = lax.axis_index("gy"), lax.axis_index("gz")
    gx = (xh * n_zz + zz) * 2 + core
    n1 = n_x * n_gz * 2
    g1 = (xh * n_gz + gz) * 2 + core

    def gx_id(index):
        return {"xh": index // (2 * n_zz), "zz": (index // 2) % n_zz, "core": index % 2}

    def g1_id(index):
        return {"xh": index // (2 * n_gz), "gz": (index // 2) % n_gz, "core": index % 2}

    gx_up, gx_dn = (gx + 1) % n_gx, (gx + n_gx - 1) % n_gx
    gy_up, gy_dn = (gy + 1) % n_gy, (gy + n_gy - 1) % n_gy

    smalls = [
        pltpu.make_async_copy(src, dst, small_sem.at[k])
        for k, (src, dst) in enumerate(
            (
                (coef_hbm, coef), (pml_hbm, pml), (eps_r_hbm, eps_r),
                (eps_l_hbm, eps_l), (ritz_hbm, ritz), (mat_hbm, mat),
            )
        )
    ]
    for copy in smalls:
        copy.start()

    for comp in (0, 2, 1):
        for c in range(2):
            pltpu.make_async_copy(
                fields.at[c, :, comp], v.at[c, :, comp], load_sem.at[comp]
            ).start()

    barrier = pltpu.get_barrier_semaphore()

    def signal(sem, device_id):
        pl.semaphore_signal(sem, inc=1, device_id=device_id, device_id_type=MESH)

    def beside(step):
        return (
            {"gy": (gy + step) % n_gy},
            {"gy": (gy + n_gy - step) % n_gy},
            {"zz": (zz + step) % n_zz},
            {"zz": (zz + n_zz - step) % n_zz},
        )

    greeted = [gx_id(gx_up), gx_id(gx_dn)] + list(beside(1))
    greeted += [g1_id((g1 + d) % n1) for d in range(1, n1)]
    for device_id in greeted:
        signal(barrier, device_id)

    def remote(src, dst, slot, device_id):
        return pltpu.make_async_remote_copy(
            src_ref=src, dst_ref=dst, send_sem=halo_send.at[slot], recv_sem=halo_recv.at[slot],
            device_id=device_id, device_id_type=MESH,
        )

    up_z = remote(fields.at[:, :, 0:2, 0], up_raw, 0, {"gz": 0})
    up_x = remote(send_x, up_xh, 1, gx_id(gx_dn))
    up_y = remote(send_y, up_yh, 2, {"gy": gy_dn})

    pl.semaphore_wait(barrier, len(greeted))

    @pl.when(gz == 1)
    def _():
        up_z.start()
        up_raw[...] = jnp.zeros(up_raw.shape, jnp.float32)

    for copy in smalls:
        copy.wait()

    for device_id in beside(1):
        signal(near, device_id)

    row16 = lax.broadcasted_iota(jnp.int32, (16, 128), 0)
    lane16 = lax.broadcasted_iota(jnp.int32, (16, 128), 1)
    lane8 = lax.broadcasted_iota(jnp.int32, (8, 128), 1)
    row8 = lax.broadcasted_iota(jnp.int32, (8, 128), 0)

    def width(slot):
        return jnp.full((8, 128), pml[slot], jnp.int32).astype(jnp.float32)

    def put(kind, places, length, low, high):
        value = inverse_stretch(places, float(length), low, high)
        sxy[kind, 0] = value[0]
        sxy[kind, 1] = value[1]

    px = (row16 + gx * nx).astype(jnp.float32)
    py = (lane16 + gy * ny).astype(jnp.float32)
    twice = lambda t: jnp.concatenate([t, t], axis=0)
    lx, hx_w, ly, hy_w = (twice(width(slot)) for slot in range(4))
    total_x, total_y, total_z = nx * n_gx, ny * n_gy, nz * n_gz
    put(0, px + 0.5, total_x, lx, hx_w)
    put(1, px, total_x, lx, hx_w)
    put(2, px + 1.0, total_x, lx, hx_w)
    put(3, py + 0.5, total_y, ly, hy_w)
    put(4, py, total_y, ly, hy_w)
    put(5, py + 1.0, total_y, ly, hy_w)
    lz, hz_w = width(4), width(5)

    def z_stretch(z, carry):
        places = jnp.full((8, 128), z + gz * nz, jnp.int32).astype(jnp.float32)
        for kind, shift in ((0, 0.5), (1, 0.0)):
            value = inverse_stretch(places + shift, float(total_z), lz, hz_w)
            sz[kind, 0, z] = value[0]
            sz[kind, 1, z] = value[1]
        return carry

    lax.fori_loop(0, nz + 1, z_stretch, 0)

    acc[...] = jnp.zeros(acc.shape, jnp.float32)
    sym[...] = jnp.zeros(sym.shape, jnp.float32)
    zero8 = jnp.zeros((8, 128), jnp.float32)

    def loaded(comp):
        pltpu.make_async_copy(fields.at[:, :, comp], v.at[:, :, comp], load_sem.at[comp]).wait()

    def combine(vr, vi, vs, b):
        both = minus = plus = None
        for a in range(NV):
            cr, ci = coef[0, a, b], coef[1, a, b]
            p, q, r = cr * vs[a], (ci - cr) * vr[a], (cr + ci) * vi[a]
            both = p if both is None else both + p
            minus = q if minus is None else minus + q
            plus = r if plus is None else plus + r
        return both - plus, both + minus

    def combined(vr, vi):
        vs = [x + y for x, y in zip(vr, vi)]
        return [combine(vr, vi, vs, b) for b in range(NV)]

    def packed_lanes(ref, comp, lane):
        tile = None
        for c in range(2):
            for a in range(NV):
                part = None
                for z in range(nz):
                    for t in range(2):
                        column = ref[c, a, comp, z, 8 * t : 8 * t + 8, lane : lane + 1]
                        column = jnp.broadcast_to(column, (8, 128))
                        place = 2 * z + t
                        part = column if part is None else jnp.where(lane_in == place, column, part)
                group = c * NV + a
                tile = part if tile is None else jnp.where(lane_group == group, part, tile)
        return tile

    lane_in, lane_group = lane8 % 16, lane8 // 16
    factors = []
    for d in range(8):
        factor = None
        for out in range(8):
            src = (out - d) % 8
            a, b = src % NV, out % NV
            if out // NV == src // NV:
                value = coef[0, a, b]
            elif out // NV == 0:
                value = -coef[1, a, b]
            else:
                value = coef[1, a, b]
            factor = (
                jnp.full((8, 128), value, jnp.float32)
                if factor is None
                else jnp.where(lane_group == out, value, factor)
            )
        factors.append(factor)
    for slot, comp in ((0, 0), (1, 2)):
        loaded(comp)
        raw = packed_lanes(v, comp, 0)
        turned = factors[0] * raw
        for d in range(1, 8):
            turned = turned + factors[d] * pltpu.roll(raw, 16 * d, 1)
        send_y[slot] = turned
    up_y.start()

    loaded(1)
    for comp in (1, 2):
        rows = [
            [
                jnp.concatenate([v[c, a, comp, z, 0:1, :] for z in range(nz)], axis=0)
                for a in range(NV)
            ]
            for c in range(2)
        ]
        for b, (re, im) in enumerate(combined(*rows)):
            send_x[0, b, comp - 1] = re
            send_x[1, b, comp - 1] = im
    up_x.start()

    def rotate(z, carry):
        for comp in range(3):
            vr = [v[0, a, comp, z] for a in range(NV)]
            vi = [v[1, a, comp, z] for a in range(NV)]
            for b, (re, im) in enumerate(combined(vr, vi)):
                basis[0, b, comp, z] = re
                basis[1, b, comp, z] = im
                if comp < 2:
                    layers[0, b, comp, z] = re
                    layers[1, b, comp, z] = im
        return carry

    lax.fori_loop(0, nz, rotate, 0)

    def pair(ref, *index):
        return ref[(0,) + index], ref[(1,) + index]

    def three(value):
        return value[0], value[1], value[0] + value[1]

    def dot3(left, right):
        sums = None
        for p, q in zip(left, right):
            terms = [x * y for x, y in zip(p, q)]
            sums = terms if sums is None else [x + y for x, y in zip(sums, terms)]
        return sums

    def local_gram(z, carry):
        m = mat[z]

        def pick(table):
            low = jnp.where(m == 0, table[0], table[1])
            return OMEGA_SQ * jnp.where(m < 2, low, jnp.where(m == 2, table[2], table[3]))

        er, ei = pick(eps_r), pick(eps_l)
        eps[0, z] = er
        eps[1, z] = ei
        for a in range(NV):
            q = [three(cmul((er, ei), pair(basis, a, comp, z))) for comp in range(3)]
            for b in range(a, NV):
                k = PAIRS.index((a, b))
                for part, value in enumerate(dot3(q, [three(pair(basis, b, comp, z)) for comp in range(3)])):
                    sym[part, k] += fold(value)
        return carry

    lax.fori_loop(0, nz, local_gram, 0)

    pl.semaphore_wait(near, 4)
    for device_id in beside(2):
        signal(far, device_id)

    up_x.wait_recv()
    up_y.wait_recv()
    pl.semaphore_wait(far, 4)
    for device_id in (beside(4)[0], beside(4)[2]):
        signal(opposite, device_id)

    @pl.when(gx == n_gx - 1)
    def _():
        up_xh[...] = jnp.zeros(up_xh.shape, jnp.float32)

    @pl.when(gy == n_gy - 1)
    def _():
        up_yh[...] = jnp.zeros(up_yh.shape, jnp.float32)

    def stretch(kind):
        return sxy[kind, 0], sxy[kind, 1]

    def stretch_z(kind, z):
        return twice(sz[kind, 0, z]), twice(sz[kind, 1, z])

    def unpacked(ref, slot, c, b, z, lane):
        parts = []
        for t in range(2):
            place = (c * NV + b) * 16 + 2 * z + t
            parts.append(pltpu.roll(ref[slot], (lane - place) % 128, 1))
        return jnp.concatenate(parts, axis=0)

    def forward(z, on_x, on_y, on_z):
        plain = not (on_x or on_y or on_z)
        sx = [stretch(k) for k in range(3)] if on_x else None
        sy = [stretch(3 + k) for k in range(3)] if on_y else None
        sz3 = [stretch_z(0, z), stretch_z(1, z), stretch_z(1, z + 1)] if on_z else None
        for b in range(NV):
            f = [pair(basis, b, comp, z) for comp in range(3)]

            def both(comp, ahead, factors3, upper=False):
                d = csub(ahead, f[comp])
                if factors3 is None:
                    return d, d
                rows = slice(8, 16) if upper else slice(0, 16)
                part = lambda value: [x[rows] for x in value]
                sh, se, se_next = (part(x) for x in factors3)
                near_part, far_part = part(f[comp]), part(ahead)
                results = cmul(sh, part(d)), csub(cmul(se_next, far_part), cmul(se, near_part))
                if not upper:
                    return results
                return tuple(
                    [jnp.concatenate([d[c][0:8], value[c]], axis=0) for c in range(2)]
                    for value in results
                )

            dx, dy, dz = {}, {}, {}
            for comp in (1, 2):
                ahead = [
                    jnp.where(
                        row16 == 15,
                        up_xh[c, b, comp - 1, pl.ds(z, 1), :],
                        pltpu.roll(f[comp][c], 15, 0),
                    )
                    for c in range(2)
                ]
                dx[comp] = both(comp, ahead, sx, on_x == "upper")
            for comp in (0, 2):
                ahead = [
                    jnp.where(
                        lane16 == 127,
                        unpacked(up_yh, comp // 2, c, b, z, 127),
                        pltpu.roll(f[comp][c], 127, 1),
                    )
                    for c in range(2)
                ]
                dy[comp] = both(comp, ahead, sy)
            for comp in (0, 1):
                dz[comp] = both(comp, pair(layers, b, comp, z + 1), sz3)
            turned = curl(*({k: x[0] for k, x in d.items()} for d in (dx, dy, dz)))
            for comp in range(3):
                for c in range(2):
                    h[c, b, comp, z] = turned[comp][c]
            if not plain:
                turned = curl(*({k: x[1] for k, x in d.items()} for d in (dx, dy, dz)))
                for comp in range(3):
                    for c, value in enumerate(three(turned[comp])):
                        gs[c, b, comp] = value
        for b in range(NV):
            hb = [three(pair(h, b, comp, z)) for comp in range(3)]
            for a in range(b + 1 if plain else NV):
                if plain:
                    ga = [three(pair(h, a, comp, z)) for comp in range(3)]
                else:
                    ga = [(gs[0, a, comp], gs[1, a, comp], gs[2, a, comp]) for comp in range(3)]
                for part, value in enumerate(dot3(ga, hb)):
                    if plain:
                        sym[part, PAIRS.index((a, b))] -= fold(value)
                    else:
                        acc[part, a, b] += fold(value)

    edge = jnp.logical_or(jnp.logical_or(gy == 0, gy == n_gy - 1), gx == 0)
    x_end = gx == n_gx - 1
    last = nz - 1

    def sweep(phase, carry):
        @pl.when(phase == 1)
        def _():
            @pl.when(gz == 0)
            def _():
                up_z.wait_recv()

            for comp in range(2):
                vr = [up_raw[0, a, comp] for a in range(NV)]
                vi = [up_raw[1, a, comp] for a in range(NV)]
                for b, (re, im) in enumerate(combined(vr, vi)):
                    layers[0, b, comp, nz] = re
                    layers[1, b, comp, nz] = im

        on_lo = (1 - phase) * ((nz - 5) * gz) + phase * last
        on_hi = (1 - phase) * (4 + (nz - 5) * gz) + phase * (last + gz)
        off_lo = (1 - phase) * (4 * (1 - gz)) + phase * last
        off_hi = (1 - phase) * (last - 4 * gz) + phase * (nz - gz)

        def run(lo, hi, *flags):
            def step(z, inner):
                forward(z, *flags)
                return inner

            lax.fori_loop(lo, hi, step, 0)

        @pl.when(edge)
        def _():
            run(phase * last, last + phase, "all", True, True)

        @pl.when(jnp.logical_not(edge))
        def _():
            for at_end, on_x in ((False, None), (True, "upper")):
                @pl.when(x_end == at_end)
                def _():
                    run(on_lo, on_hi, on_x, False, True)
                    run(off_lo, off_hi, on_x, False, False)

        return carry

    lax.fori_loop(0, 2, sweep, 0)

    tile = zero8
    for b in range(NV):
        rows = zero8
        for c in range(2):
            for a in range(NV):
                k = PAIRS.index((min(a, b), max(a, b)))
                sums = [acc[part, a, b] - sym[part, k] for part in range(3)]
                s = sums[0] - sums[1] if c == 0 else sums[2] - sums[0] - sums[1]
                s = jnp.sum(s, axis=0, keepdims=True)
                rows = jnp.where(row8 == c * NV + a, s, rows)
        total = jnp.sum(rows, axis=1, keepdims=True)
        tile = jnp.where(lane8 == NV * row8 + b, total, tile)
    tile = jnp.sum(tile, axis=0, keepdims=True)

    def exchange(buf, count, me, ids, ss, rs):
        for d in sorted(range(1, count), key=lambda d: abs(d - count // 2)):
            pltpu.make_async_remote_copy(
                src_ref=buf.at[me], dst_ref=buf.at[me], send_sem=ss, recv_sem=rs,
                device_id=ids((me + d) % count), device_id_type=MESH,
            ).start()
        others = buf.at[pl.ds(0, count - 1)]

        def arrived():
            pltpu.make_async_copy(others, others, rs).wait()
            parts = [buf[k] for k in range(count)]
            while len(parts) > 1:
                parts = [parts[k] + parts[k + 1] for k in range(0, len(parts), 2)]
            return parts[0]

        def sent():
            pltpu.make_async_copy(others, others, ss).wait()

        return arrived, sent

    buf1[g1] = tile
    arrived1, sent1 = exchange(buf1, n1, g1, g1_id, ss1, rs1)

    hsend_y[0] = packed_lanes(h, 0, 127)
    hsend_y[1] = packed_lanes(h, 2, 127)
    for c in range(2):
        for b in range(NV):
            for comp in (1, 2):
                hsend_x[c, b, comp - 1] = jnp.concatenate(
                    [h[c, b, comp, z, 15:16, :] for z in range(nz)], axis=0
                )
    dn_z = remote(h.at[:, :, 0:2, nz - 1], dn_zh, 3, {"gz": 1})
    dn_x = remote(hsend_x, dn_xh, 4, gx_id(gx_up))
    dn_y = remote(hsend_y, dn_yh, 5, {"gy": gy_up})

    @pl.when(gz == 0)
    def _():
        dn_z.start()

    dn_x.start()
    dn_y.start()

    pl.semaphore_wait(opposite, 2)
    plane = n_gy * n_zz
    buf2[gy * n_zz + zz] = arrived1()
    arrived2, sent2 = exchange(
        buf2, plane, gy * n_zz + zz, lambda k: {"gy": k // n_zz, "zz": k % n_zz}, ss2, rs2
    )

    dn_x.wait_recv()
    dn_y.wait_recv()

    @pl.when(gz == 1)
    def _():
        dn_z.wait_recv()

    @pl.when(gz == 0)
    def _():
        dn_zh[...] = jnp.zeros(dn_zh.shape, jnp.float32)

    @pl.when(gx == 0)
    def _():
        dn_xh[...] = jnp.zeros(dn_xh.shape, jnp.float32)

    @pl.when(gy == 0)
    def _():
        dn_yh[...] = jnp.zeros(dn_yh.shape, jnp.float32)

    def backward(z, behind_z):
        er, ei = eps[0, z], eps[1, z]
        for b in range(NV):
            f = [pair(h, b, comp, z) for comp in range(3)]
            dx, dy, dz = {}, {}, {}
            for comp in (1, 2):
                behind = tuple(
                    jnp.where(
                        row16 == 0,
                        dn_xh[c, b, comp - 1, pl.ds(z, 1), :],
                        pltpu.roll(f[comp][c], 1, 0),
                    )
                    for c in range(2)
                )
                dx[comp] = cmul(stretch(1), csub(f[comp], behind))
            for comp in (0, 2):
                behind = tuple(
                    jnp.where(
                        lane16 == 0,
                        unpacked(dn_yh, comp // 2, c, b, z, 128),
                        pltpu.roll(f[comp][c], 1, 1),
                    )
                    for c in range(2)
                )
                dy[comp] = cmul(stretch(4), csub(f[comp], behind))
            for comp in (0, 1):
                dz[comp] = cmul(stretch_z(1, z), csub(f[comp], behind_z(b, comp)))
            turned = curl(dx, dy, dz)
            shifted = (er + ritz[0, b], ei + ritz[1, b])
            for comp in range(3):
                out = csub(turned[comp], cmul(shifted, pair(basis, b, comp, z)))
                resid[0, b, comp, z] = out[0]
                resid[1, b, comp, z] = out[1]

    backward(0, lambda b, comp: pair(dn_zh, b, comp))

    def backward_step(z, carry):
        backward(z, lambda b, comp: pair(h, b, comp, z - 1))
        return carry

    lax.fori_loop(1, nz, backward_step, 0)

    @pl.when(gz == 1)
    def _():
        up_z.wait_send()

    @pl.when(gz == 0)
    def _():
        dn_z.wait_send()

    for copy in (up_x, up_y, dn_x, dn_y):
        copy.wait_send()
    sent1()
    final = arrived2() * (1.0 / (3.0 * total_x * total_y * total_z))
    final = jnp.broadcast_to(final, (8, 128))
    spread = final
    for r in range(1, 2 * NV):
        spread = jnp.where(row8 == r, pltpu.roll(final, 128 - NV * r, 1), spread)
    gram[0] = spread[0:NV, 0:NV]
    gram[1] = spread[NV : 2 * NV, 0:NV]
    sent2()


def write_out(basis, resid, gram, basis_out, resid_out, gram_out, sem):
    copies = [pltpu.make_async_copy(gram, gram_out, sem.at[16])]
    for k in range(8):
        c, a = k // 4, k % 4
        copies.append(pltpu.make_async_copy(basis.at[c, a], basis_out.at[c, a], sem.at[2 * k]))
        copies.append(pltpu.make_async_copy(resid.at[c, a], resid_out.at[c, a], sem.at[2 * k + 1]))
    for copy in copies:
        copy.start()
    for copy in copies:
        copy.wait()


def body(sizes, fields, material, pml_width, eps_real, eps_loss, coeffs, ritz):
    nz, nx, ny, n_gx, n_gy, n_gz, n_zz = sizes
    n1 = n_gx // n_zz * n_gz
    whole = fields.shape
    f32 = jnp.float32
    vmem = pl.BlockSpec(memory_space=pltpu.VMEM)
    face_x = pltpu.VMEM((2, NV, 2, nz, ny), f32)
    face_y = pltpu.VMEM((2, 8, 128), f32)
    face_z = pltpu.VMEM((2, NV, 2, nx, ny), f32)
    dma = pltpu.SemaphoreType.DMA
    made = pl.pallas_call(
        functools.partial(kernel, sizes),
        out_shape=(
            jax.ShapeDtypeStruct(whole, f32),
            jax.ShapeDtypeStruct(whole, f32),
            jax.ShapeDtypeStruct((2, NV, NV), f32),
        ),
        in_specs=[pl.BlockSpec(memory_space=pltpu.HBM)] * 7,
        out_specs=(vmem, vmem, vmem),
        scratch_shapes=[
            pltpu.SMEM((6,), jnp.int32),
            pltpu.SMEM((4,), f32),
            pltpu.SMEM((4,), f32),
            pltpu.SMEM((2, NV, NV), f32),
            pltpu.SMEM((2, NV), f32),
            pltpu.VMEM((nz, nx, ny), jnp.int32),
            pltpu.VMEM(whole, f32),
            pltpu.VMEM(whole, f32),
            pltpu.VMEM((3, NV, 3, nx, ny), f32),
            pltpu.VMEM((3, NV, NV, 8, 128), f32),
            pltpu.VMEM((3, len(PAIRS), 8, 128), f32),
            pltpu.VMEM((2, nz, nx, ny), f32),
            pltpu.VMEM((6, 2, nx, ny), f32),
            pltpu.VMEM((2, 2, nz + 1, 8, 128), f32),
            face_x, face_y, face_x, face_y, face_z,
            pltpu.VMEM((2, NV, 2, nz + 1, nx, ny), f32),
            face_x, face_y, face_x, face_y, face_z,
            pltpu.VMEM((n1, 1, 128), f32),
            pltpu.VMEM((n_gy * n_zz, 1, 128), f32),
            dma((6,)),
            dma((3,)),
            dma((6,)),
            dma((6,)),
            dma, dma, dma, dma,
            pltpu.SemaphoreType.REGULAR,
            pltpu.SemaphoreType.REGULAR,
            pltpu.SemaphoreType.REGULAR,
        ],
        compiler_params=pltpu.CompilerParams(
            collective_id=0, has_side_effects=True, vmem_limit_bytes=24 * 1024 * 1024
        ),
    )(*(pltpu.with_memory_space_constraint(x, pltpu.HBM) for x in (pml_width, eps_real, eps_loss, coeffs, ritz, material, fields)))
    hbm = pl.BlockSpec(memory_space=pltpu.HBM)
    return pl.pallas_call(
        write_out,
        out_shape=tuple(jax.ShapeDtypeStruct(x.shape, f32) for x in made),
        in_specs=[vmem] * 3,
        out_specs=(hbm,) * 3,
        scratch_shapes=[dma((17,))],
        compiler_params=pltpu.CompilerParams(vmem_limit_bytes=1024 * 1024),
    )(*made)


def solution(mesh):
    n_gx, n_gy, n_gz = mesh.shape["gx"], mesh.shape["gy"], mesh.shape["gz"]
    n_zz = n_gx // 4
    split = Mesh(
        mesh.devices.reshape(2, n_zz, 2, n_gy, n_gz),
        ("xh", "zz", "core", "gy", "gz"),
    )
    sizes = (16 // n_gz, 512 // n_gx, 1024 // n_gy, n_gx, n_gy, n_gz, n_zz)
    placed = (P(None, None, None, "gz", GX, "gy"), P("gz", GX, "gy"), P(), P(), P(), P(), P())
    return jax.shard_map(
        functools.partial(body, sizes),
        mesh=split,
        in_specs=placed,
        out_specs=(P(None, None, None, "gz", GX, "gy"), P(None, None, None, "gz", GX, "gy"), P()),
        check_vma=False,
    )
```

```python
import functools

import jax
import jax.numpy as jnp
from jax import lax
from jax.experimental import pallas as pl
from jax.experimental.pallas import tpu as pltpu
from jax.sharding import Mesh
from jax.sharding import PartitionSpec as P

GX = ("xh", "zz", "core")
OMEGA_SQ = 0.36
SIGMA_TOP = 3.0
NV = 4
MESH = pl.DeviceIdType.MESH
PAIRS = [(a, b) for a in range(NV) for b in range(a, NV)]


def inverse_stretch(places, length, low_width, high_width):
    inside_depth = jnp.clip((low_width - places) / low_width, 0.0, 1.0) + jnp.clip(
        (places + 1.0 - length + high_width) / high_width, 0.0, 1.0
    )
    absorb = SIGMA_TOP * inside_depth * inside_depth
    scaled = 1.0 / (1.0 + absorb * absorb)
    return scaled, -absorb * scaled


def cmul(f, v):
    return (f[0] * v[0] - f[1] * v[1], f[0] * v[1] + f[1] * v[0])


def csub(p, q):
    return (p[0] - q[0], p[1] - q[1])


def curl(dx, dy, dz):
    return (
        csub(dy[2], dz[1]),
        csub(dz[0], dx[2]),
        csub(dx[1], dy[0]),
    )


def fold(x):
    return x[0:8] + x[8:16]


def kernel(
    sizes,
    pml_hbm, eps_r_hbm, eps_l_hbm, coef_hbm, ritz_hbm, mat_hbm, fields,
    basis, resid, gram,
    pml, eps_r, eps_l, coef, ritz, mat, v, h, gs, acc, sym, eps, sxy, sz,
    send_x, send_y, up_xh, up_yh, up_raw, layers,
    hsend_x, hsend_y, dn_xh, dn_yh, dn_zh,
    buf1, buf2,
    small_sem, load_sem, halo_send, halo_recv, ss1, rs1, ss2, rs2, near, far, opposite,
):
    nz, nx, ny, n_gx, n_gy, n_gz, n_zz = sizes
    n_x = n_gx // (2 * n_zz)
    xh, zz, core = (lax.axis_index(name) for name in GX)
    gy, gz = lax.axis_index("gy"), lax.axis_index("gz")
    gx = (xh * n_zz + zz) * 2 + core
    n1 = n_x * n_gz * 2
    g1 = (xh * n_gz + gz) * 2 + core

    def gx_id(index):
        return {
            "xh": lax.div(index, 2 * n_zz),
            "zz": lax.rem(lax.div(index, 2), n_zz),
            "core": lax.rem(index, 2),
        }

    def g1_id(index):
        return {
            "xh": lax.div(index, 2 * n_gz),
            "gz": lax.rem(lax.div(index, 2), n_gz),
            "core": lax.rem(index, 2),
        }

    gx_up, gx_dn = lax.rem(gx + 1, n_gx), lax.rem(gx + n_gx - 1, n_gx)
    gy_up, gy_dn = lax.rem(gy + 1, n_gy), lax.rem(gy + n_gy - 1, n_gy)

    smalls = [
        pltpu.make_async_copy(src, dst, small_sem.at[k])
        for k, (src, dst) in enumerate(
            (
                (coef_hbm, coef), (pml_hbm, pml), (eps_r_hbm, eps_r),
                (eps_l_hbm, eps_l), (ritz_hbm, ritz), (mat_hbm, mat),
            )
        )
    ]
    for copy in smalls:
        copy.start()

    for comp in (0, 2, 1):
        for c in range(2):
            pltpu.make_async_copy(
                fields.at[c, :, comp], v.at[c, :, comp], load_sem.at[comp]
            ).start()

    barrier = pltpu.get_barrier_semaphore()

    def signal(sem, device_id):
        pl.semaphore_signal(sem, inc=1, device_id=device_id, device_id_type=MESH)

    def beside(step):
        return (
            {"gy": lax.rem(gy + step, n_gy)},
            {"gy": lax.rem(gy + n_gy - step, n_gy)},
            {"zz": lax.rem(zz + step, n_zz)},
            {"zz": lax.rem(zz + n_zz - step, n_zz)},
        )

    greeted = [gx_id(gx_up), gx_id(gx_dn)] + list(beside(1))
    greeted += [g1_id(lax.rem(g1 + d, n1)) for d in range(1, n1)]
    for device_id in greeted:
        signal(barrier, device_id)

    def remote(src, dst, slot, device_id):
        return pltpu.make_async_remote_copy(
            src_ref=src, dst_ref=dst, send_sem=halo_send.at[slot], recv_sem=halo_recv.at[slot],
            device_id=device_id, device_id_type=MESH,
        )

    up_z = remote(fields.at[:, :, 0:2, 0], up_raw, 0, {"gz": 0})
    up_x = remote(send_x, up_xh, 1, gx_id(gx_dn))
    up_y = remote(send_y, up_yh, 2, {"gy": gy_dn})

    pl.semaphore_wait(barrier, len(greeted))

    @pl.when(gz == 1)
    def _():
        up_z.start()
        up_raw[...] = jnp.zeros(up_raw.shape, jnp.float32)

    for copy in smalls:
        copy.wait()

    for device_id in beside(1):
        signal(near, device_id)

    row16 = lax.broadcasted_iota(jnp.int32, (16, 128), 0)
    lane16 = lax.broadcasted_iota(jnp.int32, (16, 128), 1)
    lane8 = lax.broadcasted_iota(jnp.int32, (8, 128), 1)
    row8 = lax.broadcasted_iota(jnp.int32, (8, 128), 0)

    def width(slot):
        return jnp.full((8, 128), pml[slot], jnp.int32).astype(jnp.float32)

    def put(kind, places, length, low, high):
        value = inverse_stretch(places, float(length), low, high)
        sxy[kind, 0] = value[0]
        sxy[kind, 1] = value[1]

    px = (row16 + gx * nx).astype(jnp.float32)
    py = (lane16 + gy * ny).astype(jnp.float32)
    twice = lambda t: jnp.concatenate([t, t], axis=0)
    lx, hx_w, ly, hy_w = (twice(width(slot)) for slot in range(4))
    total_x, total_y, total_z = nx * n_gx, ny * n_gy, nz * n_gz
    put(0, px + 0.5, total_x, lx, hx_w)
    put(1, px, total_x, lx, hx_w)
    put(2, px + 1.0, total_x, lx, hx_w)
    put(3, py + 0.5, total_y, ly, hy_w)
    put(4, py, total_y, ly, hy_w)
    put(5, py + 1.0, total_y, ly, hy_w)
    lz, hz_w = width(4), width(5)

    def z_stretch(z, carry):
        places = jnp.full((8, 128), z + gz * nz, jnp.int32).astype(jnp.float32)
        for kind, shift in ((0, 0.5), (1, 0.0)):
            value = inverse_stretch(places + shift, float(total_z), lz, hz_w)
            sz[kind, 0, z] = value[0]
            sz[kind, 1, z] = value[1]
        return carry

    lax.fori_loop(0, nz + 1, z_stretch, 0)

    acc[...] = jnp.zeros(acc.shape, jnp.float32)
    sym[...] = jnp.zeros(sym.shape, jnp.float32)
    zero8 = jnp.zeros((8, 128), jnp.float32)

    def loaded(comp):
        pltpu.make_async_copy(fields.at[:, :, comp], v.at[:, :, comp], load_sem.at[comp]).wait()

    def combine(vr, vi, vs, b):
        both = minus = plus = None
        for a in range(NV):
            cr, ci = coef[0, a, b], coef[1, a, b]
            p, q, r = cr * vs[a], (ci - cr) * vr[a], (cr + ci) * vi[a]
            both = p if both is None else both + p
            minus = q if minus is None else minus + q
            plus = r if plus is None else plus + r
        return both - plus, both + minus

    def combined(vr, vi):
        vs = [x + y for x, y in zip(vr, vi)]
        return [combine(vr, vi, vs, b) for b in range(NV)]

    def packed_lanes(ref, comp, lane):
        tile = None
        for c in range(2):
            for a in range(NV):
                part = None
                for z in range(nz):
                    for t in range(2):
                        column = ref[c, a, comp, z, 8 * t : 8 * t + 8, lane : lane + 1]
                        column = jnp.broadcast_to(column, (8, 128))
                        place = 2 * z + t
                        part = column if part is None else jnp.where(lane_in == place, column, part)
                group = c * NV + a
                tile = part if tile is None else jnp.where(lane_group == group, part, tile)
        return tile

    lane_in, lane_group = lane8 % 16, lane8 // 16
    factors = []
    for d in range(8):
        factor = None
        for out in range(8):
            src = (out - d) % 8
            a, b = src % NV, out % NV
            if out // NV == src // NV:
                value = coef[0, a, b]
            elif out // NV == 0:
                value = -coef[1, a, b]
            else:
                value = coef[1, a, b]
            factor = (
                jnp.full((8, 128), value, jnp.float32)
                if factor is None
                else jnp.where(lane_group == out, value, factor)
            )
        factors.append(factor)
    for slot, comp in ((0, 0), (1, 2)):
        loaded(comp)
        raw = packed_lanes(v, comp, 0)
        turned = factors[0] * raw
        for d in range(1, 8):
            turned = turned + factors[d] * pltpu.roll(raw, 16 * d, 1)
        send_y[slot] = turned
    up_y.start()

    loaded(1)
    for comp in (1, 2):
        rows = [
            [
                jnp.concatenate([v[c, a, comp, z, 0:1, :] for z in range(nz)], axis=0)
                for a in range(NV)
            ]
            for c in range(2)
        ]
        for b, (re, im) in enumerate(combined(*rows)):
            send_x[0, b, comp - 1] = re
            send_x[1, b, comp - 1] = im
    up_x.start()

    def rotate(z, carry):
        for comp in range(3):
            vr = [v[0, a, comp, z] for a in range(NV)]
            vi = [v[1, a, comp, z] for a in range(NV)]
            for b, (re, im) in enumerate(combined(vr, vi)):
                basis[0, b, comp, z] = re
                basis[1, b, comp, z] = im
                if comp < 2:
                    layers[0, b, comp, z] = re
                    layers[1, b, comp, z] = im
        return carry

    lax.fori_loop(0, nz, rotate, 0)

    pl.semaphore_wait(near, 4)
    for device_id in beside(2):
        signal(far, device_id)

    def pair(ref, *index):
        return ref[(0,) + index], ref[(1,) + index]

    def three(value):
        return value[0], value[1], value[0] + value[1]

    def dot3(left, right):
        sums = None
        for p, q in zip(left, right):
            terms = [x * y for x, y in zip(p, q)]
            sums = terms if sums is None else [x + y for x, y in zip(sums, terms)]
        return sums

    def local_gram(z, carry):
        m = mat[z]

        def pick(table):
            low = jnp.where(m == 0, table[0], table[1])
            return OMEGA_SQ * jnp.where(m < 2, low, jnp.where(m == 2, table[2], table[3]))

        er, ei = pick(eps_r), pick(eps_l)
        eps[0, z] = er
        eps[1, z] = ei
        for a in range(NV):
            q = [three(cmul((er, ei), pair(basis, a, comp, z))) for comp in range(3)]
            for b in range(a, NV):
                k = PAIRS.index((a, b))
                for part, value in enumerate(dot3(q, [three(pair(basis, b, comp, z)) for comp in range(3)])):
                    sym[part, k] += fold(value)
        return carry

    lax.fori_loop(0, nz, local_gram, 0)


    up_x.wait_recv()
    up_y.wait_recv()

    @pl.when(gx == n_gx - 1)
    def _():
        up_xh[...] = jnp.zeros(up_xh.shape, jnp.float32)

    @pl.when(gy == n_gy - 1)
    def _():
        up_yh[...] = jnp.zeros(up_yh.shape, jnp.float32)

    def stretch(kind):
        return sxy[kind, 0], sxy[kind, 1]

    def stretch_z(kind, z):
        return twice(sz[kind, 0, z]), twice(sz[kind, 1, z])

    def unpacked(ref, slot, c, b, z, lane):
        parts = []
        for t in range(2):
            place = (c * NV + b) * 16 + 2 * z + t
            parts.append(pltpu.roll(ref[slot], (lane - place) % 128, 1))
        return jnp.concatenate(parts, axis=0)

    def forward(z, on_x, on_y, on_z):
        plain = not (on_x or on_y or on_z)
        sx = [stretch(k) for k in range(3)] if on_x else None
        sy = [stretch(3 + k) for k in range(3)] if on_y else None
        sz3 = [stretch_z(0, z), stretch_z(1, z), stretch_z(1, z + 1)] if on_z else None
        for b in range(NV):
            f = [pair(basis, b, comp, z) for comp in range(3)]

            def both(comp, ahead, factors3, upper=False):
                d = csub(ahead, f[comp])
                if factors3 is None:
                    return d, d
                rows = slice(8, 16) if upper else slice(0, 16)
                part = lambda value: [x[rows] for x in value]
                sh, se, se_next = (part(x) for x in factors3)
                near_part, far_part = part(f[comp]), part(ahead)
                results = cmul(sh, part(d)), csub(cmul(se_next, far_part), cmul(se, near_part))
                if not upper:
                    return results
                return tuple(
                    [jnp.concatenate([d[c][0:8], value[c]], axis=0) for c in range(2)]
                    for value in results
                )

            dx, dy, dz = {}, {}, {}
            for comp in (1, 2):
                ahead = [
                    jnp.where(
                        row16 == 15,
                        up_xh[c, b, comp - 1, pl.ds(z, 1), :],
                        pltpu.roll(f[comp][c], 15, 0),
                    )
                    for c in range(2)
                ]
                dx[comp] = both(comp, ahead, sx, on_x == "upper")
            for comp in (0, 2):
                ahead = [
                    jnp.where(
                        lane16 == 127,
                        unpacked(up_yh, comp // 2, c, b, z, 127),
                        pltpu.roll(f[comp][c], 127, 1),
                    )
                    for c in range(2)
                ]
                dy[comp] = both(comp, ahead, sy)
            for comp in (0, 1):
                dz[comp] = both(comp, pair(layers, b, comp, z + 1), sz3)
            turned = curl(*({k: x[0] for k, x in d.items()} for d in (dx, dy, dz)))
            for comp in range(3):
                for c in range(2):
                    h[c, b, comp, z] = turned[comp][c]
            if not plain:
                turned = curl(*({k: x[1] for k, x in d.items()} for d in (dx, dy, dz)))
                for comp in range(3):
                    for c, value in enumerate(three(turned[comp])):
                        gs[c, b, comp] = value
        for b in range(NV):
            hb = [three(pair(h, b, comp, z)) for comp in range(3)]
            for a in range(b + 1 if plain else NV):
                if plain:
                    ga = [three(pair(h, a, comp, z)) for comp in range(3)]
                else:
                    ga = [(gs[0, a, comp], gs[1, a, comp], gs[2, a, comp]) for comp in range(3)]
                for part, value in enumerate(dot3(ga, hb)):
                    if plain:
                        sym[part, PAIRS.index((a, b))] -= fold(value)
                    else:
                        acc[part, a, b] += fold(value)

    edge = jnp.logical_or(jnp.logical_or(gy == 0, gy == n_gy - 1), gx == 0)
    x_end = gx == n_gx - 1
    last = nz - 1

    def sweep(phase, carry):
        @pl.when(phase == 1)
        def _():
            pl.semaphore_wait(far, 4)
            for device_id in (beside(4)[0], beside(4)[2]):
                signal(opposite, device_id)

            @pl.when(gz == 0)
            def _():
                up_z.wait_recv()

            for comp in range(2):
                vr = [up_raw[0, a, comp] for a in range(NV)]
                vi = [up_raw[1, a, comp] for a in range(NV)]
                for b, (re, im) in enumerate(combined(vr, vi)):
                    layers[0, b, comp, nz] = re
                    layers[1, b, comp, nz] = im

        on_lo = (1 - phase) * ((nz - 5) * gz) + phase * last
        on_hi = (1 - phase) * (4 + (nz - 5) * gz) + phase * (last + gz)
        off_lo = (1 - phase) * (4 * (1 - gz)) + phase * last
        off_hi = (1 - phase) * (last - 4 * gz) + phase * (nz - gz)

        def run(lo, hi, *flags):
            def step(z, inner):
                forward(z, *flags)
                return inner

            lax.fori_loop(lo, hi, step, 0)

        @pl.when(edge)
        def _():
            run(phase * last, last + phase, "all", True, True)

        @pl.when(jnp.logical_not(edge))
        def _():
            for at_end, on_x in ((False, None), (True, "upper")):
                @pl.when(x_end == at_end)
                def _():
                    run(on_lo, on_hi, on_x, False, True)
                    run(off_lo, off_hi, on_x, False, False)

        return carry

    lax.fori_loop(0, 2, sweep, 0)

    tile = zero8
    for b in range(NV):
        rows = zero8
        for c in range(2):
            for a in range(NV):
                k = PAIRS.index((min(a, b), max(a, b)))
                sums = [acc[part, a, b] - sym[part, k] for part in range(3)]
                s = sums[0] - sums[1] if c == 0 else sums[2] - sums[0] - sums[1]
                s = jnp.sum(s, axis=0, keepdims=True)
                rows = jnp.where(row8 == c * NV + a, s, rows)
        total = jnp.sum(rows, axis=1, keepdims=True)
        tile = jnp.where(lane8 == NV * row8 + b, total, tile)
    tile = jnp.sum(tile, axis=0, keepdims=True)

    def exchange(buf, count, me, ids, ss, rs):
        for k in range(count - 1):
            pltpu.make_async_remote_copy(
                src_ref=buf.at[me], dst_ref=buf.at[me], send_sem=ss, recv_sem=rs,
                device_id=ids(k + (me <= k).astype(jnp.int32)), device_id_type=MESH,
            ).start()
        others = buf.at[pl.ds(0, count - 1)]

        def arrived():
            pltpu.make_async_copy(others, others, rs).wait()
            parts = [buf[k] for k in range(count)]
            while len(parts) > 1:
                parts = [parts[k] + parts[k + 1] for k in range(0, len(parts), 2)]
            return parts[0]

        def sent():
            pltpu.make_async_copy(others, others, ss).wait()

        return arrived, sent

    buf1[g1] = tile
    arrived1, sent1 = exchange(buf1, n1, g1, g1_id, ss1, rs1)

    hsend_y[0] = packed_lanes(h, 0, 127)
    hsend_y[1] = packed_lanes(h, 2, 127)
    for c in range(2):
        for b in range(NV):
            for comp in (1, 2):
                hsend_x[c, b, comp - 1] = jnp.concatenate(
                    [h[c, b, comp, z, 15:16, :] for z in range(nz)], axis=0
                )
    dn_z = remote(h.at[:, :, 0:2, nz - 1], dn_zh, 3, {"gz": 1})
    dn_x = remote(hsend_x, dn_xh, 4, gx_id(gx_up))
    dn_y = remote(hsend_y, dn_yh, 5, {"gy": gy_up})

    @pl.when(gz == 0)
    def _():
        dn_z.start()

    dn_x.start()
    dn_y.start()

    pl.semaphore_wait(opposite, 2)
    plane = n_gy * n_zz
    buf2[gy * n_zz + zz] = arrived1()
    arrived2, sent2 = exchange(
        buf2, plane, gy * n_zz + zz, lambda k: {"gy": lax.div(k, n_zz), "zz": lax.rem(k, n_zz)}, ss2, rs2
    )

    dn_x.wait_recv()
    dn_y.wait_recv()

    @pl.when(gz == 1)
    def _():
        dn_z.wait_recv()

    @pl.when(gz == 0)
    def _():
        dn_zh[...] = jnp.zeros(dn_zh.shape, jnp.float32)

    @pl.when(gx == 0)
    def _():
        dn_xh[...] = jnp.zeros(dn_xh.shape, jnp.float32)

    @pl.when(gy == 0)
    def _():
        dn_yh[...] = jnp.zeros(dn_yh.shape, jnp.float32)

    def backward(z, behind_z):
        er, ei = eps[0, z], eps[1, z]
        for b in range(NV):
            f = [pair(h, b, comp, z) for comp in range(3)]
            dx, dy, dz = {}, {}, {}
            for comp in (1, 2):
                behind = tuple(
                    jnp.where(
                        row16 == 0,
                        dn_xh[c, b, comp - 1, pl.ds(z, 1), :],
                        pltpu.roll(f[comp][c], 1, 0),
                    )
                    for c in range(2)
                )
                dx[comp] = cmul(stretch(1), csub(f[comp], behind))
            for comp in (0, 2):
                behind = tuple(
                    jnp.where(
                        lane16 == 0,
                        unpacked(dn_yh, comp // 2, c, b, z, 128),
                        pltpu.roll(f[comp][c], 1, 1),
                    )
                    for c in range(2)
                )
                dy[comp] = cmul(stretch(4), csub(f[comp], behind))
            for comp in (0, 1):
                dz[comp] = cmul(stretch_z(1, z), csub(f[comp], behind_z(b, comp)))
            turned = curl(dx, dy, dz)
            shifted = (er + ritz[0, b], ei + ritz[1, b])
            for comp in range(3):
                out = csub(turned[comp], cmul(shifted, pair(basis, b, comp, z)))
                resid[0, b, comp, z] = out[0]
                resid[1, b, comp, z] = out[1]

    backward(0, lambda b, comp: pair(dn_zh, b, comp))

    def backward_step(z, carry):
        backward(z, lambda b, comp: pair(h, b, comp, z - 1))
        return carry

    lax.fori_loop(1, nz, backward_step, 0)

    @pl.when(gz == 1)
    def _():
        up_z.wait_send()

    @pl.when(gz == 0)
    def _():
        dn_z.wait_send()

    for copy in (up_x, up_y, dn_x, dn_y):
        copy.wait_send()
    sent1()
    final = arrived2() * (1.0 / (3.0 * total_x * total_y * total_z))
    final = jnp.broadcast_to(final, (8, 128))
    spread = final
    for r in range(1, 2 * NV):
        spread = jnp.where(row8 == r, pltpu.roll(final, 128 - NV * r, 1), spread)
    gram[0] = spread[0:NV, 0:NV]
    gram[1] = spread[NV : 2 * NV, 0:NV]
    sent2()


def write_out(basis, resid, gram, basis_out, resid_out, gram_out, sem):
    copies = [pltpu.make_async_copy(gram, gram_out, sem.at[16])]
    for k in range(8):
        c, a = k // 4, k % 4
        copies.append(pltpu.make_async_copy(basis.at[c, a], basis_out.at[c, a], sem.at[2 * k]))
        copies.append(pltpu.make_async_copy(resid.at[c, a], resid_out.at[c, a], sem.at[2 * k + 1]))
    for copy in copies:
        copy.start()
    for copy in copies:
        copy.wait()


def body(sizes, fields, material, pml_width, eps_real, eps_loss, coeffs, ritz):
    nz, nx, ny, n_gx, n_gy, n_gz, n_zz = sizes
    n1 = n_gx // n_zz * n_gz
    whole = fields.shape
    f32 = jnp.float32
    vmem = pl.BlockSpec(memory_space=pltpu.VMEM)
    face_x = pltpu.VMEM((2, NV, 2, nz, ny), f32)
    face_y = pltpu.VMEM((2, 8, 128), f32)
    face_z = pltpu.VMEM((2, NV, 2, nx, ny), f32)
    dma = pltpu.SemaphoreType.DMA
    made = pl.pallas_call(
        functools.partial(kernel, sizes),
        out_shape=(
            jax.ShapeDtypeStruct(whole, f32),
            jax.ShapeDtypeStruct(whole, f32),
            jax.ShapeDtypeStruct((2, NV, NV), f32),
        ),
        in_specs=[pl.BlockSpec(memory_space=pltpu.HBM)] * 7,
        out_specs=(vmem, vmem, vmem),
        scratch_shapes=[
            pltpu.SMEM((6,), jnp.int32),
            pltpu.SMEM((4,), f32),
            pltpu.SMEM((4,), f32),
            pltpu.SMEM((2, NV, NV), f32),
            pltpu.SMEM((2, NV), f32),
            pltpu.VMEM((nz, nx, ny), jnp.int32),
            pltpu.VMEM(whole, f32),
            pltpu.VMEM(whole, f32),
            pltpu.VMEM((3, NV, 3, nx, ny), f32),
            pltpu.VMEM((3, NV, NV, 8, 128), f32),
            pltpu.VMEM((3, len(PAIRS), 8, 128), f32),
            pltpu.VMEM((2, nz, nx, ny), f32),
            pltpu.VMEM((6, 2, nx, ny), f32),
            pltpu.VMEM((2, 2, nz + 1, 8, 128), f32),
            face_x, face_y, face_x, face_y, face_z,
            pltpu.VMEM((2, NV, 2, nz + 1, nx, ny), f32),
            face_x, face_y, face_x, face_y, face_z,
            pltpu.VMEM((n1, 1, 128), f32),
            pltpu.VMEM((n_gy * n_zz, 1, 128), f32),
            dma((6,)),
            dma((3,)),
            dma((6,)),
            dma((6,)),
            dma, dma, dma, dma,
            pltpu.SemaphoreType.REGULAR,
            pltpu.SemaphoreType.REGULAR,
            pltpu.SemaphoreType.REGULAR,
        ],
        compiler_params=pltpu.CompilerParams(
            collective_id=0, has_side_effects=True, vmem_limit_bytes=24 * 1024 * 1024
        ),
    )(*(pltpu.with_memory_space_constraint(x, pltpu.HBM) for x in (pml_width, eps_real, eps_loss, coeffs, ritz, material, fields)))
    hbm = pl.BlockSpec(memory_space=pltpu.HBM)
    return pl.pallas_call(
        write_out,
        out_shape=tuple(jax.ShapeDtypeStruct(x.shape, f32) for x in made),
        in_specs=[vmem] * 3,
        out_specs=(hbm,) * 3,
        scratch_shapes=[dma((17,))],
        compiler_params=pltpu.CompilerParams(vmem_limit_bytes=1024 * 1024),
    )(*made)


def solution(mesh):
    n_gx, n_gy, n_gz = mesh.shape["gx"], mesh.shape["gy"], mesh.shape["gz"]
    n_zz = n_gx // 4
    split = Mesh(
        mesh.devices.reshape(2, n_zz, 2, n_gy, n_gz),
        ("xh", "zz", "core", "gy", "gz"),
    )
    sizes = (16 // n_gz, 512 // n_gx, 1024 // n_gy, n_gx, n_gy, n_gz, n_zz)
    placed = (P(None, None, None, "gz", GX, "gy"), P("gz", GX, "gy"), P(), P(), P(), P(), P())
    return jax.shard_map(
        functools.partial(body, sizes),
        mesh=split,
        in_specs=placed,
        out_specs=(P(None, None, None, "gz", GX, "gy"), P(None, None, None, "gz", GX, "gy"), P()),
        check_vma=False,
    )
```
